256 devices in a mesh: row: 16 (over x, y), col: 16 (over z, core).
Axes of the slice: x: 4, y: 4, z: 8, core: 2. Of those that a mesh axis runs over, the one named last changes fastest.
Arguments:
- mobility: float32 [18432, 18432], P('row', 'col'), as said below
Outputs:
- factored: float32 [18432, 18432], P('row', 'col')
Inputs may be any that keep to these rules, and one draw needn't show every extreme that they name: `mobility`: the matrix is exactly symmetric; its block at the global indices 0 to 767 is positive definite with all eigenvalues 1 or more; the rest is a random symmetric stand-in.
All inputs are finite; a program needn't handle non-finite values.
Results may differ from the reference program's by a relative error of at most 0.00005.
Values sent between devices are 32-bit elements; how exact they have to be, the bound alone decides.
A program may use at most 128 MiB of HBM per device.

```python
import jax
import jax.numpy as jnp
import numpy as np
from jax import lax

N = 18432
B = 768
TILE = 128
N_ROW = 16
N_COL = 16


def draw_mobility(key, part):
    first, second, third = jax.random.split(key, 3)
    basis = jax.random.normal(first, (B, B), jnp.float32)
    square = jnp.dot(basis, basis.T, precision=lax.Precision.HIGHEST) / B + jnp.eye(B, dtype=jnp.float32)
    side = 0.1 * jax.random.normal(second, (N - B, B), jnp.float32)
    bulk = jax.random.normal(third, (N, N), jnp.float32)
    whole = 0.5 * (bulk + bulk.T)
    whole = whole.at[:B, :B].set(square)
    whole = whole.at[B:, :B].set(side)
    whole = whole.at[:B, B:].set(side.T)
    whole = whole.reshape(N // (N_ROW * TILE), N_ROW, TILE, N).transpose(1, 0, 2, 3).reshape(N, N)
    whole = whole.reshape(N, N // (N_COL * TILE), N_COL, TILE).transpose(0, 2, 1, 3).reshape(N, N)
    return whole


def setup_inputs(seed: int = 0) -> dict:
    arg_keys = jax.random.split(jax.random.key(seed), 2)
    return {
        "mobility": draw_mobility(jax.random.fold_in(arg_keys[1], 71), 0),
    }


def stored_positions(count):
    global_index = np.arange(B)
    tile_number = global_index // TILE
    return tile_number % count * (N // count) + tile_number // count * TILE + global_index % TILE

def reference(mobility):
    rows_at = stored_positions(N_ROW)
    cols_at = stored_positions(N_COL)
    panel_left_raw = mobility[:, cols_at]
    panel_top_raw = mobility[rows_at, :]
    square = panel_left_raw[rows_at, :]
    factor = jnp.linalg.cholesky(square)
    panel_left = lax.linalg.triangular_solve(factor, panel_left_raw, left_side=False, lower=True, transpose_a=True)
    panel_top = lax.linalg.triangular_solve(factor, panel_top_raw, left_side=True, lower=True)
    update = mobility - jnp.dot(panel_left.astype(jnp.float32), panel_top.astype(jnp.float32), precision=lax.Precision.HIGHEST, preferred_element_type=jnp.float32)
    return update.at[:, cols_at].set(panel_left)
```

```python
import functools

import jax
import jax.numpy as jnp
from jax import lax
from jax.experimental import pallas as pl
from jax.experimental.pallas import tpu as pltpu
from jax.sharding import PartitionSpec as P

B = 768
T = 128
NB = B // T
NX, NY = 4, 4
NZ = 8
R = NX * NY
C = NZ * 2
F = jnp.float32
BF = jnp.bfloat16
MESH = pl.DeviceIdType.MESH
HIGHEST = lax.Precision.HIGHEST


def dot(a, b):
    return lax.dot_general(a, b, (((1,), (0,)), ((), ())), precision=HIGHEST, preferred_element_type=F)


def dot_t(a, b):
    return lax.dot_general(a, b, (((0,), (0,)), ((), ())), precision=HIGHEST, preferred_element_type=F)


def factor_diag(d_ref, v_ref):
    sub = lax.broadcasted_iota(jnp.int32, (8, T), 0)
    lane = lax.broadcasted_iota(jnp.int32, (8, T), 1)

    def wide(x):
        return jnp.broadcast_to(x, (8, T))

    count = T // 8
    a = [d_ref[8 * q : 8 * q + 8, :] for q in range(count)]
    v = [jnp.where(lane == sub + 8 * q, 1.0, 0.0).astype(F) for q in range(count)]
    for p in range(count):
        c = [wide(a[p][:, 8 * p + i : 8 * p + i + 1]) for i in range(8)]
        wa, wv, fv, scale = a[p], v[p], v[p], None
        for i in range(8):
            pivot = wide(c[i][i : i + 1, :])
            inverse = 1.0 / pivot
            m = c[i] * inverse
            here = sub == i
            for k in range(i + 1, 8):
                row = wide(c[k][i : i + 1, :])
                c[k] = jnp.where(here, row * inverse, c[k] - m * row)
            if p < count - 1:
                row = wide(wa[i : i + 1, :])
                wa = jnp.where(here, row * inverse, wa - m * row)
                row = wide(wv[i : i + 1, :])
                wv = jnp.where(here, row * inverse, wv - m * row)
            row = wide(fv[i : i + 1, :])
            fv = fv - jnp.where(sub > i, m, 0.0) * row
            root = lax.rsqrt(pivot)
            scale = root if scale is None else jnp.where(here, root, scale)
        v_ref[8 * p : 8 * p + 8, :] = fv * scale
        if p == count - 1:
            break
        rows_a = [wide(wa[i : i + 1, :]) for i in range(8)]
        rows_v = [wide(wv[i : i + 1, :]) for i in range(8)]
        for q in range(p + 1, count):
            co = [wide(a[q][:, 8 * p + i : 8 * p + i + 1]) for i in range(8)]
            for i in range(8):
                a[q] = a[q] - co[i] * rows_a[i]
                v[q] = v[q] - co[i] * rows_v[i]


def remote(src, dst, send, recv, device):
    return pltpu.make_async_remote_copy(
        src_ref=src, dst_ref=dst, send_sem=send, recv_sem=recv, device_id=device, device_id_type=MESH
    )


def gather_kernel(
    mob, top, left, y_ref, sq, u_scr, d_scr, v_scr,
    as_, ar, bs, br, cs, cr, sts, str_, sls, slr, loc, t1s, t1r, t2s, t2r, us, ur, ds, dr, ws, wr,
):
    row, col = lax.axis_index("row"), lax.axis_index("col")
    x, y = row // NY, row % NY
    z, core = col // 2, col % 2
    other = z * 2 + 1 - core
    piece = mob.shape[0] // C

    barrier = pltpu.get_barrier_semaphore()

    @pl.loop(0, R)
    def _(i):
        @pl.when(i != row)
        def _():
            pl.semaphore_signal(barrier, inc=1, device_id=(i, col), device_id_type=MESH)

    @pl.loop(0, C)
    def _(i):
        @pl.when(i != col)
        def _():
            pl.semaphore_signal(barrier, inc=1, device_id=(row, i), device_id_type=MESH)

    pl.semaphore_wait(barrier, R + C - 2)

    def a_copy(to, slot, half):
        return remote(
            mob.at[0:T, 0:T], sq.at[half, pl.ds(row_at(row), T), pl.ds(pl.multiple_of(slot * T, T), T)],
            as_.at[to], ar.at[slot], (row, to * 2 + half),
        )

    def row_at(r):
        return pl.multiple_of(r * T, T)

    a_sender = jnp.logical_and(row < NB, jnp.logical_and(col < NB, col >= row))

    def a_local():
        slot = col // 2
        return pltpu.make_async_copy(
            mob.at[0:T, 0:T],
            sq.at[core, pl.ds(row_at(row), T), pl.ds(pl.multiple_of(slot * T, T), T)], ar.at[slot],
        )

    @pl.when(a_sender)
    def _():
        a_local().start()

        @pl.loop(0, NZ)
        def _(to):
            @pl.when(to != z)
            def _():
                a_copy(to, col // 2, core).start()

    def top_piece(i):
        return remote(
            mob.at[pl.ds(pl.multiple_of(i * 8, 8), 8), :], top.at[row, i // NY, i % NY], sts.at[i], str_.at[row], (i, col)
        )

    def top_own():
        return pltpu.make_async_copy(
            mob.at[pl.ds(pl.multiple_of(row * 8, 8), 8), :], top.at[row, x, y], loc.at[0]
        )

    def left_piece(i):
        return remote(
            mob.at[pl.ds(pl.multiple_of(i * piece, 8), piece), 0:T],
            left.at[i, :, pl.ds(pl.multiple_of(col * T, T), T)], sls.at[i], slr.at[col], (row, i),
        )

    def left_own():
        return pltpu.make_async_copy(
            mob.at[pl.ds(pl.multiple_of(col * piece, 8), piece), 0:T],
            left.at[col, :, pl.ds(pl.multiple_of(col * T, T), T)], loc.at[1],
        )

    def b_copy(r, slot, to):
        ref = sq.at[core, pl.ds(r * T, T), pl.ds(slot * T, T)]
        return remote(ref, ref, bs.at[slot, to], br.at[r, slot], (to, col))

    def c_copy(half, r, slot):
        ref = sq.at[half, pl.ds(r * T, T), pl.ds(slot * T, T)]
        return remote(ref, ref, cs.at[r, slot], cr.at[r, slot], (row, other))

    for r in range(NB):
        @pl.when(row == r)
        def _():
            for slot in range(NB // 2):
                @pl.when(2 * slot + core >= r)
                def _():
                    a_copy(z, slot, core).wait_recv()

                    @pl.loop(0, R)
                    def _(to):
                        @pl.when(to != row)
                        def _():
                            b_copy(r, slot, to).start()

    @pl.when(row < NB)
    def _():
        top_own().start()

        @pl.loop(0, R)
        def _(i):
            @pl.when(i != row)
            def _():
                top_piece(i).start()

    @pl.when(col < NB)
    def _():
        left_own().start()

        @pl.loop(0, C)
        def _(i):
            @pl.when(i != col)
            def _():
                left_piece(i).start()

    def swap_strip(r):
        for slot in range(NB // 2):
            @pl.when(2 * slot + core >= r)
            def _():
                @pl.when(row != r)
                def _():
                    b_copy(r, slot, row).wait_recv()

                c_copy(core, r, slot).start()

    def wait_strip(r):
        for slot in range(NB // 2):
            @pl.when(2 * slot + 1 - core >= r)
            def _():
                c_copy(1 - core, r, slot).wait_recv()

    def wait_scatter():
        for g in range(NB):
            @pl.when(row != g)
            def _():
                remote(top.at[g, x, y], top.at[g, x, y], sts.at[0], str_.at[g], (row, col)).wait_recv()

            @pl.when(col != g)
            def _():
                ref = left.at[col, :, pl.ds(g * T, T)]
                remote(ref, ref, sls.at[0], slr.at[g], (row, col)).wait_recv()

        @pl.when(row < NB)
        def _():
            top_own().wait()

        @pl.when(col < NB)
        def _():
            left_own().wait()

    H = NB // 2

    def t1(axis, src, to):
        if axis == 0:
            ref, dev = top.at[0:H, src, y], (to * NY + y, col)
        else:
            ref, dev = top.at[H:NB, x, src], (x * NY + to, col)
        return remote(ref, ref, t1s.at[axis, to], t1r.at[axis, src], dev)

    def t2(axis, src, to):
        if axis == 0:
            ref, dev = top.at[0:H, :, src], (x * NY + to, col)
        else:
            ref, dev = top.at[H:NB, src], (to * NY + y, col)
        return remote(ref, ref, t2s.at[axis, to], t2r.at[axis, src], dev)

    def spread(make, mine):
        for axis in range(2):
            for to in range(4):
                @pl.when(to != mine[axis])
                def _():
                    make(axis, mine[axis], to).start()

    def collect(make, mine, send):
        for axis in range(2):
            for to in range(4):
                @pl.when(to != mine[axis])
                def _():
                    if send:
                        make(axis, mine[axis], to).wait_send()
                    else:
                        make(axis, to, mine[axis]).wait_recv()

    def up(step, at):
        ref = left.at[(at - step + NZ) % NZ * 2 + core]
        return remote(ref, ref, us.at[step], ur.at[step], (row, (z + 1) % NZ * 2 + core))

    def down(step, at):
        ref = left.at[(at + step) % NZ * 2 + core]
        return remote(ref, ref, ds.at[step], dr.at[step], (row, (z + NZ - 1) % NZ * 2 + core))

    UP, DOWN = 4, 3

    def swap(which, half, zz):
        ref = left.at[zz * 2 + half]
        return remote(ref, ref, ws.at[which], wr.at[which], (row, other))

    def set_of(which):
        if which <= UP:
            return (z - which + NZ) % NZ
        return (z + which - UP) % NZ

    def hop(step):
        if step > 0:
            up(step - 1, (z - 1 + NZ) % NZ).wait_recv()
            swap(step, core, set_of(step)).start()
            if step - 1 < DOWN:
                down(step - 1, (z + 1) % NZ).wait_recv()
                swap(UP + step, core, set_of(UP + step)).start()
        else:
            swap(0, core, z).start()
        if step < UP:
            up(step, z).start()
        if step < DOWN:
            down(step, z).start()

    y_ref[...] = jnp.zeros_like(y_ref)
    swap_strip(0)

    def tile(r, c):
        return sq.at[c % 2, pl.ds(r * T, T), pl.ds(c // 2 * T, T)]

    @pl.loop(0, NB)
    def _(k):
        for kk in range(NB):
            lo, hi = kk * T, kk * T + T

            @pl.when(k == kk)
            def _():
                wait_strip(kk)
                if kk == 0:
                    d_scr[...] = tile(0, 0)[...]
                else:
                    w = u_scr[:lo, lo:hi]
                    d_scr[...] = tile(kk, kk)[...] - dot_t(w, u_scr[:lo, lo:hi])
                if kk + 1 < NB:
                    swap_strip(kk + 1)
                if kk == 0:
                    wait_scatter()
                    spread(t1, (x, y))
                if kk == 1:
                    collect(t1, (x, y), False)
                    spread(t2, (y, x))
                if kk <= UP:
                    hop(kk)

        factor_diag(d_scr, v_scr)
        for kk in range(NB):
            lo, hi = kk * T, kk * T + T

            @pl.when(k == kk)
            def _():
                inverse = v_scr[...]
                y_ref[lo:hi, lo:hi] = inverse
                if kk > 0:
                    w = u_scr[:lo, lo:hi]
                    y_ref[lo:hi, :lo] = -dot(inverse, dot_t(w, y_ref[:lo, :lo]))
                if hi < B:
                    r = jnp.concatenate([tile(kk, c)[...] for c in range(kk + 1, NB)], axis=1)
                    if kk > 0:
                        r = r - dot_t(w, u_scr[:lo, hi:])
                    u_scr[lo:hi, hi:] = dot(inverse, r)

    collect(t2, (y, x), False)
    for which in range(NZ):
        swap(which, 1 - core, set_of(which)).wait_recv()

    @pl.when(a_sender)
    def _():
        @pl.loop(0, NZ)
        def _(to):
            @pl.when(to != z)
            def _():
                a_copy(to, col // 2, core).wait_send()

    for r in range(NB):
        @pl.when(row == r)
        def _():
            for slot in range(NB // 2):
                @pl.when(2 * slot + core >= r)
                def _():
                    @pl.loop(0, R)
                    def _(to):
                        @pl.when(to != row)
                        def _():
                            b_copy(r, slot, to).wait_send()

        for slot in range(NB // 2):
            @pl.when(2 * slot + core >= r)
            def _():
                c_copy(core, r, slot).wait_send()

    @pl.when(row < NB)
    def _():
        @pl.loop(0, R)
        def _(i):
            @pl.when(i != row)
            def _():
                top_piece(i).wait_send()

    @pl.when(col < NB)
    def _():
        @pl.loop(0, C)
        def _(i):
            @pl.when(i != col)
            def _():
                left_piece(i).wait_send()

    collect(t1, (x, y), True)
    collect(t2, (y, x), True)
    for step in range(UP):
        up(step, z).wait_send()
    for step in range(DOWN):
        down(step, z).wait_send()
    for which in range(NZ):
        swap(which, core, set_of(which)).wait_send()


def gather(mobility):
    rows, cols = mobility.shape
    D = pltpu.SemaphoreType.DMA
    top, left, inverse = pl.pallas_call(
        gather_kernel,
        out_shape=(
            jax.ShapeDtypeStruct((NB, NX, NY, T // R, cols), F),
            jax.ShapeDtypeStruct((C, rows // C, B), F),
            jax.ShapeDtypeStruct((B, B), F),
        ),
        in_specs=[pl.BlockSpec(memory_space=pl.ANY)],
        out_specs=(
            pl.BlockSpec(memory_space=pl.ANY),
            pl.BlockSpec(memory_space=pl.ANY),
            pl.BlockSpec(memory_space=pltpu.VMEM),
        ),
        scratch_shapes=[
            pltpu.VMEM((2, B, B // 2), F),
            pltpu.VMEM((B, B), F),
            pltpu.VMEM((T, T), F),
            pltpu.VMEM((T, T), F),
            D((NZ,)), D((NB // 2,)),
            D((NB // 2, R)), D((NB, NB // 2)),
            D((NB, NB // 2)), D((NB, NB // 2)),
            D((R,)), D((NB,)), D((C,)), D((NB,)), D((2,)),
            D((2, 4)), D((2, 4)), D((2, 4)), D((2, 4)),
            D((4,)), D((4,)), D((3,)), D((3,)), D((NZ,)), D((NZ,)),
        ],
        compiler_params=pltpu.CompilerParams(
            collective_id=0, has_side_effects=True, vmem_limit_bytes=32 << 20
        ),
    )(mobility)
    return top.reshape(B, cols), left.reshape(rows, B), inverse


def halves(x):
    high = x.astype(BF)
    return high, (x - high.astype(F)).astype(BF)


def update_kernel(steps, mob, left, top, inv, out, i3, t3, xl):
    m = pl.program_id(0)
    BLK = 256

    @pl.when(m == 0)
    def _():
        high, low = halves(inv[...])
        i3[0] = high
        i3[1] = low
        for b in range(B // BLK):
            high, low = halves(top[b * BLK : (b + 1) * BLK, :])
            t3[b * BLK : (b + 1) * BLK, :] = high
            t3[B + b * BLK : B + (b + 1) * BLK, :] = low
        for b in reversed(range(B // BLK)):
            lo, hi = b * BLK, (b + 1) * BLK
            ih, il = i3[0, lo:hi, :hi], i3[1, lo:hi, :hi]
            th, tl = t3[:hi, :], t3[B : B + hi, :]
            s = jnp.dot(ih, th, preferred_element_type=F)
            s += jnp.dot(ih, tl, preferred_element_type=F)
            s += jnp.dot(il, th, preferred_element_type=F)
            high, low = halves(s)
            t3[lo:hi, :] = high
            t3[B + lo : B + hi, :] = low

    lh, ll = halves(left[...])
    dims = (((1,), (1,)), ((), ()))
    for b in range(B // BLK):
        lo, hi = b * BLK, (b + 1) * BLK
        ih, il = i3[0, lo:hi, :hi], i3[1, lo:hi, :hi]
        s = lax.dot_general(lh[:, :hi], ih, dims, preferred_element_type=F)
        s += lax.dot_general(lh[:, :hi], il, dims, preferred_element_type=F)
        s += lax.dot_general(ll[:, :hi], ih, dims, preferred_element_type=F)
        xl[:, lo:hi] = s
    xh, xo = halves(xl[...])
    th, tl = t3[:B, :], t3[B:, :]
    s = jnp.dot(xh, th, preferred_element_type=F)
    s += jnp.dot(xh, tl, preferred_element_type=F)
    s += jnp.dot(xo, th, preferred_element_type=F)
    out[...] = mob[...] - s
    col = lax.axis_index("col")

    @pl.when(col < NB)
    def _():
        out[:, 0:T] = xl[:, pl.ds(pl.multiple_of(jnp.minimum(col, NB - 1) * T, T), T)]


def update(mobility, left, top, inverse):
    rows, cols = mobility.shape
    steps = 6
    tm = rows // steps
    return pl.pallas_call(
        functools.partial(update_kernel, steps),
        grid=(steps,),
        out_shape=jax.ShapeDtypeStruct(mobility.shape, F),
        in_specs=[
            pl.BlockSpec((tm, cols), lambda i: (i, 0)),
            pl.BlockSpec((tm, B), lambda i: (i, 0)),
            pl.BlockSpec((B, cols), lambda i: (0, 0)),
            pl.BlockSpec((B, B), lambda i: (0, 0)),
        ],
        out_specs=pl.BlockSpec((tm, cols), lambda i: (i, 0)),
        scratch_shapes=[
            pltpu.VMEM((2, B, B), BF),
            pltpu.VMEM((2 * B, cols), BF),
            pltpu.VMEM((tm, B), F),
        ],
        compiler_params=pltpu.CompilerParams(vmem_limit_bytes=48 << 20),
    )(mobility, left, top, inverse)


def on_device(mobility):
    top, left, inverse = gather(mobility)
    return update(mobility, left, top, inverse)


def solution(mesh):
    return jax.shard_map(
        on_device,
        mesh=mesh,
        in_specs=(P("row", "col"),),
        out_specs=P("row", "col"),
        check_vma=False,
    )
```

```python
import functools

import jax
import jax.numpy as jnp
from jax import lax
from jax.experimental import pallas as pl
from jax.experimental.pallas import tpu as pltpu
from jax.sharding import PartitionSpec as P

B = 768
T = 128
NB = B // T
NX, NY = 4, 4
NZ = 8
R = NX * NY
C = NZ * 2
F = jnp.float32
BF = jnp.bfloat16
MESH = pl.DeviceIdType.MESH
HIGHEST = lax.Precision.HIGHEST


def dot(a, b):
    return lax.dot_general(a, b, (((1,), (0,)), ((), ())), precision=HIGHEST, preferred_element_type=F)


def dot_t(a, b):
    return lax.dot_general(a, b, (((0,), (0,)), ((), ())), precision=HIGHEST, preferred_element_type=F)


def factor_diag(d_ref, v_ref, between):
    sub = lax.broadcasted_iota(jnp.int32, (8, T), 0)

    def wide(x):
        return jnp.broadcast_to(x, (8, T))

    count, group = T // 8, T // 16
    eye = lax.broadcasted_iota(jnp.int32, (T, T), 0) == lax.broadcasted_iota(jnp.int32, (T, T), 1)
    v_ref[...] = jnp.where(eye, 1.0, 0.0).astype(F)
    for first in range(0, count, group):
        end = first + group
        last = end == count
        a = {q: d_ref[8 * q : 8 * q + 8, :] for q in range(first, end)}
        v = {q: v_ref[8 * q : 8 * q + 8, :] for q in range(first, end)}
        done_a, done_v, ahead = [], [], None
        for p in range(first, end):
            c = ahead
            if c is None:
                c = [wide(a[p][:, 8 * p + i : 8 * p + i + 1]) for i in range(8)]
            near, far = p + 1 < end, p + 2 < end
            if near:
                co = [wide(a[p + 1][:, 8 * p + i : 8 * p + i + 1]) for i in range(8)]
                ahead = [wide(a[p + 1][:, 8 * p + 8 + k : 8 * p + 9 + k]) for k in range(8)]
            wa = fa = a[p]
            wv = fv = v[p]
            scale = inverses = None
            for i in range(8):
                here = sub == i
                pivot = wide(c[i][i : i + 1, :])
                inverse = 1.0 / pivot
                m = jnp.where(here, 0.0, c[i]) * inverse
                below = jnp.where(sub > i, c[i], 0.0) * inverse
                for k in range(i + 1, 8):
                    c[k] = c[k] - m * wide(c[k][i : i + 1, :])
                row_a, row_v = wide(fa[i : i + 1, :]), wide(fv[i : i + 1, :])
                if near:
                    t = co[i] * inverse
                    for k in range(8):
                        ahead[k] = ahead[k] - t * wide(co[i][k : k + 1, :])
                    a[p + 1] = a[p + 1] - t * row_a
                    v[p + 1] = v[p + 1] - t * row_v
                    for k in range(i + 1, 8):
                        co[k] = co[k] - co[i] * wide(m[k : k + 1, :])
                if far:
                    wa = wa - m * wide(wa[i : i + 1, :])
                    wv = wv - m * wide(wv[i : i + 1, :])
                fv = fv - below * row_v
                fa = fa - below * row_a
                root = lax.rsqrt(pivot)
                scale = root if scale is None else jnp.where(here, root, scale)
                inverses = inverse if inverses is None else jnp.where(here, inverse, inverses)
            fv = fv * scale
            v_ref[8 * p : 8 * p + 8, :] = fv
            if not last:
                done_a.append(fa * scale)
                done_v.append(fv)
            if not far:
                continue
            wa, wv = wa * inverses, wv * inverses
            rows_a = [wide(wa[i : i + 1, :]) for i in range(8)]
            rows_v = [wide(wv[i : i + 1, :]) for i in range(8)]
            for q in range(p + 2, end):
                cq = [wide(a[q][:, 8 * p + i : 8 * p + i + 1]) for i in range(8)]
                for i in range(8):
                    a[q] = a[q] - cq[i] * rows_a[i]
                    v[q] = v[q] - cq[i] * rows_v[i]
        if not last:
            u, w = jnp.concatenate(done_a, axis=0), jnp.concatenate(done_v, axis=0)
            r = dot_t(u, jnp.concatenate([u, w], axis=1))
            d_ref[8 * end :, :] -= r[8 * end :, :T]
            v_ref[8 * end :, :] -= r[8 * end :, T:]
            between()


def remote(src, dst, send, recv, device):
    return pltpu.make_async_remote_copy(
        src_ref=src, dst_ref=dst, send_sem=send, recv_sem=recv, device_id=device, device_id_type=MESH
    )


def gather_kernel(
    mob, top, left, y_ref, sq, u_scr, d_scr, v_scr,
    as_, ar, b1s, b2s, br, cs, cr, sts, str_, sls, slr, loc, ts, tr, us, ur, ds, dr, ws, wr,
):
    row, col = lax.axis_index("row"), lax.axis_index("col")
    x, y = row // NY, row % NY
    z, core = col // 2, col % 2
    other = z * 2 + 1 - core
    piece = mob.shape[0] // C

    barrier = pltpu.get_barrier_semaphore()

    @pl.loop(0, R)
    def _(i):
        @pl.when(i != row)
        def _():
            pl.semaphore_signal(barrier, inc=1, device_id=(i, col), device_id_type=MESH)

    @pl.loop(0, C)
    def _(i):
        @pl.when(i != col)
        def _():
            pl.semaphore_signal(barrier, inc=1, device_id=(row, i), device_id_type=MESH)

    pl.semaphore_wait(barrier, R + C - 2)

    def a_copy(to, slot, half):
        return remote(
            mob.at[0:T, 0:T], sq.at[half, pl.ds(row_at(row), T), pl.ds(pl.multiple_of(slot * T, T), T)],
            as_.at[to], ar.at[slot], (row, to * 2 + half),
        )

    def row_at(r):
        return pl.multiple_of(r * T, T)

    a_sender = jnp.logical_and(row < NB, jnp.logical_and(col < NB, col >= row))

    def a_local():
        slot = col // 2
        return pltpu.make_async_copy(
            mob.at[0:T, 0:T],
            sq.at[core, pl.ds(row_at(row), T), pl.ds(pl.multiple_of(slot * T, T), T)], ar.at[slot],
        )

    @pl.when(a_sender)
    def _():
        a_local().start()

        @pl.loop(0, NZ)
        def _(to):
            @pl.when(to != z)
            def _():
                a_copy(to, col // 2, core).start()

    def top_piece(i):
        return remote(
            mob.at[pl.ds(pl.multiple_of(i * 8, 8), 8), :], top.at[row, i // NY, i % NY], sts.at[i], str_.at[row], (i, col)
        )

    def top_own():
        return pltpu.make_async_copy(
            mob.at[pl.ds(pl.multiple_of(row * 8, 8), 8), :], top.at[row, x, y], loc.at[0]
        )

    def left_piece(i):
        return remote(
            mob.at[pl.ds(pl.multiple_of(i * piece, 8), piece), 0:T],
            left.at[i, :, pl.ds(pl.multiple_of(col * T, T), T)], sls.at[i], slr.at[col], (row, i),
        )

    def left_own():
        return pltpu.make_async_copy(
            mob.at[pl.ds(pl.multiple_of(col * piece, 8), piece), 0:T],
            left.at[col, :, pl.ds(pl.multiple_of(col * T, T), T)], loc.at[1],
        )

    @pl.when(row < NB)
    def _():
        top_own().start()

        @pl.loop(0, R)
        def _(i):
            @pl.when(i != row)
            def _():
                top_piece(i).start()

    @pl.when(col < NB)
    def _():
        left_own().start()

        @pl.loop(0, C)
        def _(i):
            @pl.when(i != col)
            def _():
                left_piece(i).start()

    def b1(r, slot, to):
        ref = sq.at[core, pl.ds(r * T, T), pl.ds(slot * T, T)]
        return remote(ref, ref, b1s.at[slot, to], br.at[r, slot], (to * NY + y, col))

    def b2(r, slot, to):
        ref = sq.at[core, pl.ds(r * T, T), pl.ds(slot * T, T)]
        return remote(ref, ref, b2s.at[r, slot, to], br.at[r, slot], (x * NY + to, col))

    def c_copy(half, r, slot):
        ref = sq.at[half, pl.ds(r * T, T), pl.ds(slot * T, T)]
        return remote(ref, ref, cs.at[r, slot], cr.at[r, slot], (row, other))

    for r in range(NB):
        @pl.when(row == r)
        def _():
            for slot in range(NB // 2):
                @pl.when(2 * slot + core >= r)
                def _():
                    a_copy(z, slot, core).wait_recv()

                    @pl.loop(0, NX)
                    def _(to):
                        @pl.when(to != x)
                        def _():
                            b1(r, slot, to).start()

    def forward(r):
        @pl.when(y == r % NY)
        def _():
            for slot in range(NB // 2):
                @pl.when(2 * slot + core >= r)
                def _():
                    @pl.when(x != r // NY)
                    def _():
                        b1(r, slot, x).wait_recv()

                    @pl.loop(0, NY)
                    def _(to):
                        @pl.when(to != y)
                        def _():
                            b2(r, slot, to).start()

    for r in range(NY):
        forward(r)

    def swap_strip(r):
        for slot in range(NB // 2):
            @pl.when(2 * slot + core >= r)
            def _():
                @pl.when(y != r % NY)
                def _():
                    b2(r, slot, y).wait_recv()

                c_copy(core, r, slot).start()

    def wait_strip(r):
        for slot in range(NB // 2):
            @pl.when(2 * slot + 1 - core >= r)
            def _():
                c_copy(1 - core, r, slot).wait_recv()

    def wait_top():
        for g in range(NB):
            @pl.when(row != g)
            def _():
                ref = top.at[g, x, y]
                remote(ref, ref, sts.at[0], str_.at[g], (row, col)).wait_recv()

        @pl.when(row < NB)
        def _():
            top_own().wait()

    def wait_left():
        for g in range(NB):
            @pl.when(col != g)
            def _():
                ref = left.at[col, :, pl.ds(g * T, T)]
                remote(ref, ref, sls.at[0], slr.at[g], (row, col)).wait_recv()

        @pl.when(col < NB)
        def _():
            left_own().wait()

    H = NB // 2
    PART = 640

    def tcopy(phase, axis, kind, at):
        src = (at + (0, 0, 3, 1)[kind]) % 4
        to = (at + (1, 3, 1, 3)[kind]) % 4
        if phase == 0:
            lanes = (slice(None), slice(None), slice(0, PART), slice(PART, None))[kind]
            ref = top.at[0:H, src, y, :, lanes] if axis == 0 else top.at[H:NB, x, src, :, lanes]
        else:
            part = (slice(None), slice(None), slice(0, 2), slice(2, 4))[kind]
            ref = top.at[0:H, part, src] if axis == 1 else top.at[H:NB, src, part]
        device = (to * NY + y, col) if axis == 0 else (x * NY + to, col)
        return remote(ref, ref, ts.at[phase, axis, kind], tr.at[phase, axis, kind], device)

    place = (x, y)

    def spread(phase, step):
        for axis in range(2):
            if step == 1:
                for kind in range(2):
                    tcopy(phase, axis, kind, (place[axis] + (3, 1)[kind]) % 4).wait_recv()
            for kind in range(2 * step, 2 * step + 2):
                tcopy(phase, axis, kind, place[axis]).start()

    def spread_end(phase):
        for axis in range(2):
            for kind in range(2, 4):
                tcopy(phase, axis, kind, (place[axis] + (0, 0, 3, 1)[kind]) % 4).wait_recv()

    def spread_sent():
        for phase in range(2):
            for axis in range(2):
                for kind in range(4):
                    tcopy(phase, axis, kind, place[axis]).wait_send()

    def up(step, at):
        ref = left.at[(at - step + NZ) % NZ * 2 + core]
        return remote(ref, ref, us.at[step], ur.at[step], (row, (z + 1) % NZ * 2 + core))

    def down(step, at):
        ref = left.at[(at + step) % NZ * 2 + core]
        return remote(ref, ref, ds.at[step], dr.at[step], (row, (z + NZ - 1) % NZ * 2 + core))

    UP, DOWN = 4, 3

    def swap(which, half, zz):
        ref = left.at[zz * 2 + half]
        return remote(ref, ref, ws.at[which], wr.at[which], (row, other))

    def set_of(which):
        if which <= UP:
            return (z - which + NZ) % NZ
        return (z + which - UP) % NZ

    def hop(step):
        if step > 0:
            up(step - 1, (z - 1 + NZ) % NZ).wait_recv()
            swap(step, core, set_of(step)).start()
            if step - 1 < DOWN:
                down(step - 1, (z + 1) % NZ).wait_recv()
                swap(UP + step, core, set_of(UP + step)).start()
        else:
            swap(0, core, z).start()
        if step < UP:
            up(step, z).start()
        if step < DOWN:
            down(step, z).start()

    y_ref[...] = jnp.zeros_like(y_ref)
    swap_strip(0)

    def tile(r, c):
        return sq.at[c % 2, pl.ds(r * T, T), pl.ds(c // 2 * T, T)]

    @pl.loop(0, NB)
    def _(k):
        for kk in range(NB):
            lo, hi = kk * T, kk * T + T

            @pl.when(k == kk)
            def _():
                wait_strip(kk)
                if kk == 0:
                    d_scr[...] = tile(0, 0)[...]
                else:
                    w = u_scr[:lo, lo:hi]
                    d_scr[...] = tile(kk, kk)[...] - dot_t(w, u_scr[:lo, lo:hi])
                if kk + 1 < NB:
                    swap_strip(kk + 1)
                if kk == 0:
                    forward(4)
                    forward(5)
                if kk == 2:
                    spread_end(0)
                    spread(1, 0)
                if kk == 4:
                    spread(1, 1)

        def between():
            for kk in range(NB):
                @pl.when(k == kk)
                def _():
                    if kk == 0:
                        wait_top()
                        spread(0, 0)
                    if kk == 1:
                        spread(0, 1)
                        wait_left()
                    if kk > 0:
                        hop(kk - 1)

        factor_diag(d_scr, v_scr, between)
        for kk in range(NB):
            lo, hi = kk * T, kk * T + T

            @pl.when(k == kk)
            def _():
                inverse = v_scr[...]
                y_ref[lo:hi, lo:hi] = inverse
                if kk > 0:
                    w = u_scr[:lo, lo:hi]
                    y_ref[lo:hi, :lo] = -dot(inverse, dot_t(w, y_ref[:lo, :lo]))
                if hi < B:
                    r = jnp.concatenate([tile(kk, c)[...] for c in range(kk + 1, NB)], axis=1)
                    if kk > 0:
                        r = r - dot_t(w, u_scr[:lo, hi:])
                    u_scr[lo:hi, hi:] = dot(inverse, r)

    spread_end(1)
    for which in range(NZ):
        swap(which, 1 - core, set_of(which)).wait_recv()

    @pl.when(a_sender)
    def _():
        @pl.loop(0, NZ)
        def _(to):
            @pl.when(to != z)
            def _():
                a_copy(to, col // 2, core).wait_send()

    for r in range(NB):
        @pl.when(row == r)
        def _():
            for slot in range(NB // 2):
                @pl.when(2 * slot + core >= r)
                def _():
                    @pl.loop(0, NX)
                    def _(to):
                        @pl.when(to != x)
                        def _():
                            b1(r, slot, to).wait_send()

        @pl.when(y == r % NY)
        def _():
            for slot in range(NB // 2):
                @pl.when(2 * slot + core >= r)
                def _():
                    @pl.loop(0, NY)
                    def _(to):
                        @pl.when(to != y)
                        def _():
                            b2(r, slot, to).wait_send()

        for slot in range(NB // 2):
            @pl.when(2 * slot + core >= r)
            def _():
                c_copy(core, r, slot).wait_send()

    @pl.when(row < NB)
    def _():
        @pl.loop(0, R)
        def _(i):
            @pl.when(i != row)
            def _():
                top_piece(i).wait_send()

    @pl.when(col < NB)
    def _():
        @pl.loop(0, C)
        def _(i):
            @pl.when(i != col)
            def _():
                left_piece(i).wait_send()

    spread_sent()
    for step in range(UP):
        up(step, z).wait_send()
    for step in range(DOWN):
        down(step, z).wait_send()
    for which in range(NZ):
        swap(which, core, set_of(which)).wait_send()


def gather(mobility):
    rows, cols = mobility.shape
    D = pltpu.SemaphoreType.DMA
    top, left, inverse = pl.pallas_call(
        gather_kernel,
        out_shape=(
            jax.ShapeDtypeStruct((NB, NX, NY, T // R, cols), F),
            jax.ShapeDtypeStruct((C, rows // C, B), F),
            jax.ShapeDtypeStruct((B, B), F),
        ),
        in_specs=[pl.BlockSpec(memory_space=pl.ANY)],
        out_specs=(
            pl.BlockSpec(memory_space=pl.ANY),
            pl.BlockSpec(memory_space=pl.ANY),
            pl.BlockSpec(memory_space=pltpu.VMEM),
        ),
        scratch_shapes=[
            pltpu.VMEM((2, B, B // 2), F),
            pltpu.VMEM((B, B), F),
            pltpu.VMEM((T, T), F),
            pltpu.VMEM((T, T), F),
            D((NZ,)), D((NB // 2,)),
            D((NB // 2, NX)), D((NB, NB // 2, NY)), D((NB, NB // 2)),
            D((NB, NB // 2)), D((NB, NB // 2)),
            D((R,)), D((NB,)), D((C,)), D((NB,)), D((2,)),
            D((2, 2, 4)), D((2, 2, 4)),
            D((4,)), D((4,)), D((3,)), D((3,)), D((NZ,)), D((NZ,)),
        ],
        compiler_params=pltpu.CompilerParams(
            collective_id=0, has_side_effects=True, vmem_limit_bytes=32 << 20
        ),
    )(mobility)
    return top.reshape(B, cols), left.reshape(rows, B), inverse


def halves(x):
    high = x.astype(BF)
    return high, (x - high.astype(F)).astype(BF)


def update_kernel(steps, mob, left, top, inv, out, i3, t3, xl):
    m = pl.program_id(0)
    BLK = 256

    @pl.when(m == 0)
    def _():
        high, low = halves(inv[...])
        i3[0] = high
        i3[1] = low
        for b in range(B // BLK):
            high, low = halves(top[b * BLK : (b + 1) * BLK, :])
            t3[b * BLK : (b + 1) * BLK, :] = high
            t3[B + b * BLK : B + (b + 1) * BLK, :] = low
        for b in reversed(range(B // BLK)):
            lo, hi = b * BLK, (b + 1) * BLK
            ih, il = i3[0, lo:hi, :hi], i3[1, lo:hi, :hi]
            th, tl = t3[:hi, :], t3[B : B + hi, :]
            s = jnp.dot(ih, th, preferred_element_type=F)
            s += jnp.dot(ih, tl, preferred_element_type=F)
            s += jnp.dot(il, th, preferred_element_type=F)
            high, low = halves(s)
            t3[lo:hi, :] = high
            t3[B + lo : B + hi, :] = low

    lh, ll = halves(left[...])
    dims = (((1,), (1,)), ((), ()))
    for b in range(B // BLK):
        lo, hi = b * BLK, (b + 1) * BLK
        ih, il = i3[0, lo:hi, :hi], i3[1, lo:hi, :hi]
        s = lax.dot_general(lh[:, :hi], ih, dims, preferred_element_type=F)
        s += lax.dot_general(lh[:, :hi], il, dims, preferred_element_type=F)
        s += lax.dot_general(ll[:, :hi], ih, dims, preferred_element_type=F)
        xl[:, lo:hi] = s
    xh, xo = halves(xl[...])
    th, tl = t3[:B, :], t3[B:, :]
    s = jnp.dot(xh, th, preferred_element_type=F)
    s += jnp.dot(xh, tl, preferred_element_type=F)
    s += jnp.dot(xo, th, preferred_element_type=F)
    out[...] = mob[...] - s
    col = lax.axis_index("col")

    @pl.when(col < NB)
    def _():
        out[:, 0:T] = xl[:, pl.ds(pl.multiple_of(jnp.minimum(col, NB - 1) * T, T), T)]


def update(mobility, left, top, inverse):
    rows, cols = mobility.shape
    steps = 6
    tm = rows // steps
    return pl.pallas_call(
        functools.partial(update_kernel, steps),
        grid=(steps,),
        out_shape=jax.ShapeDtypeStruct(mobility.shape, F),
        in_specs=[
            pl.BlockSpec((tm, cols), lambda i: (i, 0)),
            pl.BlockSpec((tm, B), lambda i: (i, 0)),
            pl.BlockSpec((B, cols), lambda i: (0, 0)),
            pl.BlockSpec((B, B), lambda i: (0, 0)),
        ],
        out_specs=pl.BlockSpec((tm, cols), lambda i: (i, 0)),
        scratch_shapes=[
            pltpu.VMEM((2, B, B), BF),
            pltpu.VMEM((2 * B, cols), BF),
            pltpu.VMEM((tm, B), F),
        ],
        compiler_params=pltpu.CompilerParams(vmem_limit_bytes=48 << 20),
    )(mobility, left, top, inverse)


def on_device(mobility):
    top, left, inverse = gather(mobility)
    return update(mobility, left, top, inverse)


def solution(mesh):
    return jax.shard_map(
        on_device,
        mesh=mesh,
        in_specs=(P("row", "col"),),
        out_specs=P("row", "col"),
        check_vma=False,
    )
```

```python
import jax
import jax.numpy as jnp
from jax import lax
from jax.experimental import pallas as pl
from jax.experimental.pallas import tpu as pltpu
from jax.sharding import PartitionSpec as P

B = 768
T = 128
NB = B // T
BLK = 256
STEPS = 3
NX, NY = 4, 4
NZ = 8
R = NX * NY
C = NZ * 2
F = jnp.float32
BF = jnp.bfloat16
MESH = pl.DeviceIdType.MESH
HIGHEST = lax.Precision.HIGHEST


def dot(a, b):
    return lax.dot_general(a, b, (((1,), (0,)), ((), ())), precision=HIGHEST, preferred_element_type=F)


def dot_t(a, b):
    return lax.dot_general(a, b, (((0,), (0,)), ((), ())), precision=HIGHEST, preferred_element_type=F)


def factor_diag(d_ref, v_ref, between):
    sub = lax.broadcasted_iota(jnp.int32, (8, T), 0)

    def wide(x):
        return jnp.broadcast_to(x, (8, T))

    count, group = T // 8, T // 16
    eye = lax.broadcasted_iota(jnp.int32, (T, T), 0) == lax.broadcasted_iota(jnp.int32, (T, T), 1)
    v_ref[...] = jnp.where(eye, 1.0, 0.0).astype(F)
    for first in range(0, count, group):
        end = first + group
        last = end == count
        a = {q: d_ref[8 * q : 8 * q + 8, :] for q in range(first, end)}
        v = {q: v_ref[8 * q : 8 * q + 8, :] for q in range(first, end)}
        done_a, done_v, ahead = [], [], None
        for p in range(first, end):
            c = ahead
            if c is None:
                c = [wide(a[p][:, 8 * p + i : 8 * p + i + 1]) for i in range(8)]
            near, far = p + 1 < end, p + 2 < end
            if near:
                co = [wide(a[p + 1][:, 8 * p + i : 8 * p + i + 1]) for i in range(8)]
                ahead = [wide(a[p + 1][:, 8 * p + 8 + k : 8 * p + 9 + k]) for k in range(8)]
            wa = fa = a[p]
            wv = fv = v[p]
            scale = inverses = None
            for i in range(8):
                here = sub == i
                pivot = wide(c[i][i : i + 1, :])
                inverse = 1.0 / pivot
                m = jnp.where(here, 0.0, c[i]) * inverse
                below = jnp.where(sub > i, c[i], 0.0) * inverse
                for k in range(i + 1, 8):
                    c[k] = c[k] - m * wide(c[k][i : i + 1, :])
                row_a, row_v = wide(fa[i : i + 1, :]), wide(fv[i : i + 1, :])
                if near:
                    t = co[i] * inverse
                    for k in range(8):
                        ahead[k] = ahead[k] - t * wide(co[i][k : k + 1, :])
                    a[p + 1] = a[p + 1] - t * row_a
                    v[p + 1] = v[p + 1] - t * row_v
                    for k in range(i + 1, 8):
                        co[k] = co[k] - co[i] * wide(m[k : k + 1, :])
                if far:
                    wa = wa - m * wide(wa[i : i + 1, :])
                    wv = wv - m * wide(wv[i : i + 1, :])
                fv = fv - below * row_v
                fa = fa - below * row_a
                root = lax.rsqrt(pivot)
                scale = root if scale is None else jnp.where(here, root, scale)
                inverses = inverse if inverses is None else jnp.where(here, inverse, inverses)
            fv = fv * scale
            v_ref[8 * p : 8 * p + 8, :] = fv
            if not last:
                done_a.append(fa * scale)
                done_v.append(fv)
            if not far:
                continue
            wa, wv = wa * inverses, wv * inverses
            rows_a = [wide(wa[i : i + 1, :]) for i in range(8)]
            rows_v = [wide(wv[i : i + 1, :]) for i in range(8)]
            for q in range(p + 2, end):
                cq = [wide(a[q][:, 8 * p + i : 8 * p + i + 1]) for i in range(8)]
                for i in range(8):
                    a[q] = a[q] - cq[i] * rows_a[i]
                    v[q] = v[q] - cq[i] * rows_v[i]
        if not last:
            u, w = jnp.concatenate(done_a, axis=0), jnp.concatenate(done_v, axis=0)
            r = dot_t(u, jnp.concatenate([u, w], axis=1))
            d_ref[8 * end :, :] -= r[8 * end :, :T]
            v_ref[8 * end :, :] -= r[8 * end :, T:]
            between()


def remote(src, dst, send, recv, device):
    return pltpu.make_async_remote_copy(
        src_ref=src, dst_ref=dst, send_sem=send, recv_sem=recv, device_id=device, device_id_type=MESH
    )


def halves(x):
    high = x.astype(BF)
    return high, (x - high.astype(F)).astype(BF)


def panel_kernel(
    mob, out, top, left, y_ref, sq, u_scr, d_scr, v_scr, buf, i3, t3, xl,
    as_, ar, b1s, b2s, br, cs, cr, sts, str_, sls, slr, loc, ts, tr, us, ur, ds, dr, ws, wr, os_,
):
    row, col = lax.axis_index("row"), lax.axis_index("col")
    x, y = row // NY, row % NY
    z, core = col // 2, col % 2
    other = z * 2 + 1 - core
    piece = mob.shape[0] // C

    barrier = pltpu.get_barrier_semaphore()

    @pl.loop(0, R)
    def _(i):
        @pl.when(i != row)
        def _():
            pl.semaphore_signal(barrier, inc=1, device_id=(i, col), device_id_type=MESH)

    @pl.loop(0, C)
    def _(i):
        @pl.when(i != col)
        def _():
            pl.semaphore_signal(barrier, inc=1, device_id=(row, i), device_id_type=MESH)

    pl.semaphore_wait(barrier, R + C - 2)

    def a_copy(to, slot, half):
        return remote(
            mob.at[0:T, 0:T], sq.at[half, pl.ds(row_at(row), T), pl.ds(pl.multiple_of(slot * T, T), T)],
            as_.at[to], ar.at[slot], (row, to * 2 + half),
        )

    def row_at(r):
        return pl.multiple_of(r * T, T)

    a_sender = jnp.logical_and(row < NB, jnp.logical_and(col < NB, col >= row))

    def a_local():
        slot = col // 2
        return pltpu.make_async_copy(
            mob.at[0:T, 0:T],
            sq.at[core, pl.ds(row_at(row), T), pl.ds(pl.multiple_of(slot * T, T), T)], ar.at[slot],
        )

    @pl.when(a_sender)
    def _():
        a_local().start()

        @pl.loop(0, NZ)
        def _(to):
            @pl.when(to != z)
            def _():
                a_copy(to, col // 2, core).start()

    def top_piece(i):
        return remote(
            mob.at[pl.ds(pl.multiple_of(i * 8, 8), 8), :], top.at[row, i // NY, i % NY], sts.at[i], str_.at[row], (i, col)
        )

    def top_own():
        return pltpu.make_async_copy(
            mob.at[pl.ds(pl.multiple_of(row * 8, 8), 8), :], top.at[row, x, y], loc.at[0]
        )

    def left_piece(i):
        return remote(
            mob.at[pl.ds(pl.multiple_of(i * piece, 8), piece), 0:T],
            left.at[i, :, pl.ds(pl.multiple_of(col * T, T), T)], sls.at[i], slr.at[col], (row, i),
        )

    def left_own():
        return pltpu.make_async_copy(
            mob.at[pl.ds(pl.multiple_of(col * piece, 8), piece), 0:T],
            left.at[col, :, pl.ds(pl.multiple_of(col * T, T), T)], loc.at[1],
        )

    @pl.when(row < NB)
    def _():
        top_own().start()

        @pl.loop(0, R)
        def _(i):
            @pl.when(i != row)
            def _():
                top_piece(i).start()

    @pl.when(col < NB)
    def _():
        left_own().start()

        @pl.loop(0, C)
        def _(i):
            @pl.when(i != col)
            def _():
                left_piece(i).start()

    def b1(r, slot, to):
        ref = sq.at[core, pl.ds(r * T, T), pl.ds(slot * T, T)]
        return remote(ref, ref, b1s.at[slot, to], br.at[r, slot], (to * NY + y, col))

    def b2(r, slot, to):
        ref = sq.at[core, pl.ds(r * T, T), pl.ds(slot * T, T)]
        return remote(ref, ref, b2s.at[r, slot, to], br.at[r, slot], (x * NY + to, col))

    def c_copy(half, r, slot):
        ref = sq.at[half, pl.ds(r * T, T), pl.ds(slot * T, T)]
        return remote(ref, ref, cs.at[r, slot], cr.at[r, slot], (row, other))

    for r in range(NB):
        @pl.when(row == r)
        def _():
            for slot in range(NB // 2):
                @pl.when(2 * slot + core >= r)
                def _():
                    a_copy(z, slot, core).wait_recv()

                    @pl.loop(0, NX)
                    def _(to):
                        @pl.when(to != x)
                        def _():
                            b1(r, slot, to).start()

    def forward(r):
        @pl.when(y == r % NY)
        def _():
            for slot in range(NB // 2):
                @pl.when(2 * slot + core >= r)
                def _():
                    @pl.when(x != r // NY)
                    def _():
                        b1(r, slot, x).wait_recv()

                    @pl.loop(0, NY)
                    def _(to):
                        @pl.when(to != y)
                        def _():
                            b2(r, slot, to).start()

    for r in range(NY):
        forward(r)

    pltpu.make_async_copy(mob, buf, loc.at[2]).start()

    def swap_strip(r):
        for slot in range(NB // 2):
            @pl.when(2 * slot + core >= r)
            def _():
                @pl.when(y != r % NY)
                def _():
                    b2(r, slot, y).wait_recv()

                c_copy(core, r, slot).start()

    def wait_strip(r):
        for slot in range(NB // 2):
            @pl.when(2 * slot + 1 - core >= r)
            def _():
                c_copy(1 - core, r, slot).wait_recv()

    def wait_top():
        for g in range(NB):
            @pl.when(row != g)
            def _():
                ref = top.at[g, x, y]
                remote(ref, ref, sts.at[0], str_.at[g], (row, col)).wait_recv()

        @pl.when(row < NB)
        def _():
            top_own().wait()

    def wait_left():
        for g in range(NB):
            @pl.when(col != g)
            def _():
                ref = left.at[col, :, pl.ds(g * T, T)]
                remote(ref, ref, sls.at[0], slr.at[g], (row, col)).wait_recv()

        @pl.when(col < NB)
        def _():
            left_own().wait()

    H = NB // 2
    PART = 640

    def tcopy(phase, axis, kind, at):
        src = (at + (0, 0, 3, 1)[kind]) % 4
        to = (at + (1, 3, 1, 3)[kind]) % 4
        if phase == 0:
            lanes = (slice(None), slice(None), slice(0, PART), slice(PART, None))[kind]
            ref = top.at[0:H, src, y, :, lanes] if axis == 0 else top.at[H:NB, x, src, :, lanes]
        else:
            part = (slice(None), slice(None), slice(0, 2), slice(2, 4))[kind]
            ref = top.at[0:H, part, src] if axis == 1 else top.at[H:NB, src, part]
        device = (to * NY + y, col) if axis == 0 else (x * NY + to, col)
        return remote(ref, ref, ts.at[phase, axis, kind], tr.at[phase, axis, kind], device)

    place = (x, y)

    def spread(phase, step):
        for axis in range(2):
            if step == 1:
                for kind in range(2):
                    tcopy(phase, axis, kind, (place[axis] + (3, 1)[kind]) % 4).wait_recv()
            for kind in range(2 * step, 2 * step + 2):
                tcopy(phase, axis, kind, place[axis]).start()

    def spread_end(phase):
        for axis in range(2):
            for kind in range(2, 4):
                tcopy(phase, axis, kind, (place[axis] + (0, 0, 3, 1)[kind]) % 4).wait_recv()

    def spread_sent():
        for phase in range(2):
            for axis in range(2):
                for kind in range(4):
                    tcopy(phase, axis, kind, place[axis]).wait_send()

    def up(step, at):
        ref = left.at[(at - step + NZ) % NZ * 2 + core]
        return remote(ref, ref, us.at[step], ur.at[step], (row, (z + 1) % NZ * 2 + core))

    def down(step, at):
        ref = left.at[(at + step) % NZ * 2 + core]
        return remote(ref, ref, ds.at[step], dr.at[step], (row, (z + NZ - 1) % NZ * 2 + core))

    UP, DOWN = 4, 3

    def swap(which, half, zz):
        ref = left.at[zz * 2 + half]
        return remote(ref, ref, ws.at[which], wr.at[which], (row, other))

    def set_of(which):
        if which <= UP:
            return (z - which + NZ) % NZ
        return (z + which - UP) % NZ

    def hop(step):
        if step > 0:
            up(step - 1, (z - 1 + NZ) % NZ).wait_recv()
            swap(step, core, set_of(step)).start()
            if step - 1 < DOWN:
                down(step - 1, (z + 1) % NZ).wait_recv()
                swap(UP + step, core, set_of(UP + step)).start()
        else:
            swap(0, core, z).start()
        if step < UP:
            up(step, z).start()
        if step < DOWN:
            down(step, z).start()

    y_ref[...] = jnp.zeros_like(y_ref)
    swap_strip(0)

    def tile(r, c):
        return sq.at[c % 2, pl.ds(r * T, T), pl.ds(c // 2 * T, T)]

    @pl.loop(0, NB)
    def _(k):
        for kk in range(NB):
            lo, hi = kk * T, kk * T + T

            @pl.when(k == kk)
            def _():
                wait_strip(kk)
                if kk == 0:
                    d_scr[...] = tile(0, 0)[...]
                else:
                    w = u_scr[:lo, lo:hi]
                    d_scr[...] = tile(kk, kk)[...] - dot_t(w, u_scr[:lo, lo:hi])
                if kk + 1 < NB:
                    swap_strip(kk + 1)
                if kk == 0:
                    forward(4)
                    forward(5)
                if kk == 2:
                    spread(0, 1)
                if kk == 3:
                    spread_end(0)
                    spread(1, 0)
                    hop(1)

        def between():
            for kk in range(NB):
                @pl.when(k == kk)
                def _():
                    if kk == 0:
                        wait_top()
                        spread(0, 0)
                    if kk == 1:
                        wait_left()
                        hop(0)
                    if kk == 4:
                        hop(2)
                    if kk == 5:
                        spread(1, 1)

        factor_diag(d_scr, v_scr, between)
        for kk in range(NB):
            lo, hi = kk * T, kk * T + T

            @pl.when(k == kk)
            def _():
                inverse = v_scr[...]
                y_ref[lo:hi, lo:hi] = inverse
                if kk > 0:
                    w = u_scr[:lo, lo:hi]
                    y_ref[lo:hi, :lo] = -dot(inverse, dot_t(w, y_ref[:lo, :lo]))
                if hi < B:
                    r = jnp.concatenate([tile(kk, c)[...] for c in range(kk + 1, NB)], axis=1)
                    if kk > 0:
                        r = r - dot_t(w, u_scr[:lo, hi:])
                    u_scr[lo:hi, hi:] = dot(inverse, r)

    pair = 2 * piece

    def rows_of(which):
        return pl.ds(pl.multiple_of(set_of(which) * pair, 8), pair)

    def solve_left(group):
        for which in group:
            swap(which, 1 - core, set_of(which)).wait_recv()
        raw = jnp.concatenate([left[pl.ds(2 * set_of(w), 2)].reshape(pair, B) for w in group], axis=0)
        lh, ll = halves(raw)
        dims = (((1,), (1,)), ((), ()))
        for b in range(B // BLK):
            lo, hi = b * BLK, (b + 1) * BLK
            ih, il = i3[0, lo:hi, :hi], i3[1, lo:hi, :hi]
            s = lax.dot_general(lh[:, :hi], ih, dims, preferred_element_type=F)
            s += lax.dot_general(lh[:, :hi], il, dims, preferred_element_type=F)
            s += lax.dot_general(ll[:, :hi], ih, dims, preferred_element_type=F)
            for n, which in enumerate(group):
                xl[rows_of(which), lo:hi] = s[n * pair : (n + 1) * pair]

    hop(3)
    high, low = halves(y_ref[...])
    i3[0] = high
    i3[1] = low
    solve_left((0, 1, 5, 2, 6))

    spread_end(1)
    for g in range(NB):
        high, low = halves(top[g].reshape(T, t3.shape[1]))
        t3[g * T : g * T + T, :] = high
        t3[B + g * T : B + g * T + T, :] = low
    for b in reversed(range(B // BLK)):
        lo, hi = b * BLK, (b + 1) * BLK
        ih, il = i3[0, lo:hi, :hi], i3[1, lo:hi, :hi]
        th, tl = t3[:hi, :], t3[B : B + hi, :]
        s = jnp.dot(ih, th, preferred_element_type=F)
        s += jnp.dot(ih, tl, preferred_element_type=F)
        s += jnp.dot(il, th, preferred_element_type=F)
        high, low = halves(s)
        t3[lo:hi, :] = high
        t3[B + lo : B + hi, :] = low
    hop(4)
    solve_left((3, 7, 4))
    pltpu.make_async_copy(mob, buf, loc.at[2]).wait()

    size = buf.shape[0] // STEPS

    def store(n):
        return pltpu.make_async_copy(
            buf.at[n * size : (n + 1) * size, :], out.at[n * size : (n + 1) * size, :], os_.at[n]
        )

    for n in range(STEPS):
        rows = slice(n * size, (n + 1) * size)
        xh, xo = halves(xl[rows, :])
        th, tl = t3[:B, :], t3[B:, :]
        s = jnp.dot(xh, th, preferred_element_type=F)
        s += jnp.dot(xh, tl, preferred_element_type=F)
        s += jnp.dot(xo, th, preferred_element_type=F)
        buf[rows, :] = buf[rows, :] - s

        @pl.when(col < NB)
        def _():
            buf[rows, 0:T] = xl[rows, pl.ds(pl.multiple_of(jnp.minimum(col, NB - 1) * T, T), T)]

        store(n).start()

    @pl.when(a_sender)
    def _():
        @pl.loop(0, NZ)
        def _(to):
            @pl.when(to != z)
            def _():
                a_copy(to, col // 2, core).wait_send()

    for r in range(NB):
        @pl.when(row == r)
        def _():
            for slot in range(NB // 2):
                @pl.when(2 * slot + core >= r)
                def _():
                    @pl.loop(0, NX)
                    def _(to):
                        @pl.when(to != x)
                        def _():
                            b1(r, slot, to).wait_send()

        @pl.when(y == r % NY)
        def _():
            for slot in range(NB // 2):
                @pl.when(2 * slot + core >= r)
                def _():
                    @pl.loop(0, NY)
                    def _(to):
                        @pl.when(to != y)
                        def _():
                            b2(r, slot, to).wait_send()

        for slot in range(NB // 2):
            @pl.when(2 * slot + core >= r)
            def _():
                c_copy(core, r, slot).wait_send()

    @pl.when(row < NB)
    def _():
        @pl.loop(0, R)
        def _(i):
            @pl.when(i != row)
            def _():
                top_piece(i).wait_send()

    @pl.when(col < NB)
    def _():
        @pl.loop(0, C)
        def _(i):
            @pl.when(i != col)
            def _():
                left_piece(i).wait_send()

    spread_sent()
    for step in range(UP):
        up(step, z).wait_send()
    for step in range(DOWN):
        down(step, z).wait_send()
    for which in range(NZ):
        swap(which, core, set_of(which)).wait_send()
    for n in range(STEPS):
        store(n).wait()


def on_device(mobility):
    rows, cols = mobility.shape
    D = pltpu.SemaphoreType.DMA
    return pl.pallas_call(
        panel_kernel,
        out_shape=jax.ShapeDtypeStruct(mobility.shape, F),
        in_specs=[pl.BlockSpec(memory_space=pl.ANY)],
        out_specs=pl.BlockSpec(memory_space=pl.ANY),
        scratch_shapes=[
            pltpu.VMEM((NB, NX, NY, T // R, cols), F),
            pltpu.VMEM((C, rows // C, B), F),
            pltpu.VMEM((B, B), F),
            pltpu.VMEM((2, B, B // 2), F),
            pltpu.VMEM((B, B), F),
            pltpu.VMEM((T, T), F),
            pltpu.VMEM((T, T), F),
            pltpu.VMEM((rows, cols), F),
            pltpu.VMEM((2, B, B), BF),
            pltpu.VMEM((2 * B, cols), BF),
            pltpu.VMEM((rows, B), F),
            D((NZ,)), D((NB // 2,)),
            D((NB // 2, NX)), D((NB, NB // 2, NY)), D((NB, NB // 2)),
            D((NB, NB // 2)), D((NB, NB // 2)),
            D((R,)), D((NB,)), D((C,)), D((NB,)), D((3,)),
            D((2, 2, 4)), D((2, 2, 4)),
            D((4,)), D((4,)), D((3,)), D((3,)), D((NZ,)), D((NZ,)), D((STEPS,)),
        ],
        compiler_params=pltpu.CompilerParams(
            collective_id=0, has_side_effects=True, vmem_limit_bytes=52 << 20
        ),
    )(mobility)


def solution(mesh):
    return jax.shard_map(
        on_device,
        mesh=mesh,
        in_specs=(P("row", "col"),),
        out_specs=P("row", "col"),
        check_vma=False,
    )
```

```python
import jax
import jax.numpy as jnp
from jax import lax
from jax.experimental import pallas as pl
from jax.experimental.pallas import tpu as pltpu
from jax.sharding import PartitionSpec as P

B = 768
T = 128
NB = B // T
BLK = 256
STEPS = 4
NX, NY = 4, 4
NZ = 8
R = NX * NY
C = NZ * 2
F = jnp.float32
BF = jnp.bfloat16
MESH = pl.DeviceIdType.MESH
HIGHEST = lax.Precision.HIGHEST


def dot(a, b):
    return lax.dot_general(a, b, (((1,), (0,)), ((), ())), precision=HIGHEST, preferred_element_type=F)


def dot_t(a, b):
    return lax.dot_general(a, b, (((0,), (0,)), ((), ())), precision=HIGHEST, preferred_element_type=F)


def factor_diag(d_ref, v_ref, between):
    sub = lax.broadcasted_iota(jnp.int32, (8, T), 0)

    def wide(x):
        return jnp.broadcast_to(x, (8, T))

    count, group = T // 8, T // 16
    eye = lax.broadcasted_iota(jnp.int32, (T, T), 0) == lax.broadcasted_iota(jnp.int32, (T, T), 1)
    v_ref[...] = jnp.where(eye, 1.0, 0.0).astype(F)
    for first in range(0, count, group):
        end = first + group
        last = end == count
        a = {q: d_ref[8 * q : 8 * q + 8, :] for q in range(first, end)}
        v = {q: v_ref[8 * q : 8 * q + 8, :] for q in range(first, end)}
        done_a, done_v, ahead = [], [], None
        for p in range(first, end):
            c = ahead
            if c is None:
                c = [wide(a[p][:, 8 * p + i : 8 * p + i + 1]) for i in range(8)]
            near, far = p + 1 < end, p + 2 < end
            if near:
                co = [wide(a[p + 1][:, 8 * p + i : 8 * p + i + 1]) for i in range(8)]
                ahead = [wide(a[p + 1][:, 8 * p + 8 + k : 8 * p + 9 + k]) for k in range(8)]
            wa = fa = a[p]
            wv = fv = v[p]
            scale = inverses = None
            for i in range(8):
                here = sub == i
                pivot = wide(c[i][i : i + 1, :])
                inverse = 1.0 / pivot
                m = jnp.where(here, 0.0, c[i]) * inverse
                below = jnp.where(sub > i, c[i], 0.0) * inverse
                for k in range(i + 1, 8):
                    c[k] = c[k] - m * wide(c[k][i : i + 1, :])
                row_a, row_v = wide(fa[i : i + 1, :]), wide(fv[i : i + 1, :])
                if near:
                    t = co[i] * inverse
                    for k in range(8):
                        ahead[k] = ahead[k] - t * wide(co[i][k : k + 1, :])
                    a[p + 1] = a[p + 1] - t * row_a
                    v[p + 1] = v[p + 1] - t * row_v
                    for k in range(i + 1, 8):
                        co[k] = co[k] - co[i] * wide(m[k : k + 1, :])
                if far:
                    wa = wa - m * wide(wa[i : i + 1, :])
                    wv = wv - m * wide(wv[i : i + 1, :])
                fv = fv - below * row_v
                fa = fa - below * row_a
                root = lax.rsqrt(pivot)
                scale = root if scale is None else jnp.where(here, root, scale)
                inverses = inverse if inverses is None else jnp.where(here, inverse, inverses)
            fv = fv * scale
            v_ref[8 * p : 8 * p + 8, :] = fv
            if not last:
                done_a.append(fa * scale)
                done_v.append(fv)
            if not far:
                continue
            wa, wv = wa * inverses, wv * inverses
            rows_a = [wide(wa[i : i + 1, :]) for i in range(8)]
            rows_v = [wide(wv[i : i + 1, :]) for i in range(8)]
            for q in range(p + 2, end):
                cq = [wide(a[q][:, 8 * p + i : 8 * p + i + 1]) for i in range(8)]
                for i in range(8):
                    a[q] = a[q] - cq[i] * rows_a[i]
                    v[q] = v[q] - cq[i] * rows_v[i]
        if not last:
            u, w = jnp.concatenate(done_a, axis=0), jnp.concatenate(done_v, axis=0)
            r = dot_t(u, jnp.concatenate([u, w], axis=1))
            d_ref[8 * end :, :] -= r[8 * end :, :T]
            v_ref[8 * end :, :] -= r[8 * end :, T:]
            between()


def remote(src, dst, send, recv, device):
    return pltpu.make_async_remote_copy(
        src_ref=src, dst_ref=dst, send_sem=send, recv_sem=recv, device_id=device, device_id_type=MESH
    )


def halves(x):
    high = x.astype(BF)
    return high, (x - high.astype(F)).astype(BF)


def panel_kernel(
    mob, t3_out, xl_out, top, left, y_ref, sq, u_scr, d_scr, v_scr, i3, t3, xl,
    as_, ar, b1s, b2s, br, cs, cr, sts, str_, sls, slr, loc, ts, tr, us, ur, ds, dr, ws, wr, os_,
):
    row, col = lax.axis_index("row"), lax.axis_index("col")
    x, y = row // NY, row % NY
    z, core = col // 2, col % 2
    other = z * 2 + 1 - core
    piece = mob.shape[0] // C

    barrier = pltpu.get_barrier_semaphore()

    @pl.loop(0, R)
    def _(i):
        @pl.when(i != row)
        def _():
            pl.semaphore_signal(barrier, inc=1, device_id=(i, col), device_id_type=MESH)

    @pl.loop(0, C)
    def _(i):
        @pl.when(i != col)
        def _():
            pl.semaphore_signal(barrier, inc=1, device_id=(row, i), device_id_type=MESH)

    pl.semaphore_wait(barrier, R + C - 2)

    def a_copy(to, slot, half):
        return remote(
            mob.at[0:T, 0:T], sq.at[half, pl.ds(row_at(row), T), pl.ds(pl.multiple_of(slot * T, T), T)],
            as_.at[to], ar.at[slot], (row, to * 2 + half),
        )

    def row_at(r):
        return pl.multiple_of(r * T, T)

    a_sender = jnp.logical_and(row < NB, jnp.logical_and(col < NB, col >= row))

    def a_local():
        slot = col // 2
        return pltpu.make_async_copy(
            mob.at[0:T, 0:T],
            sq.at[core, pl.ds(row_at(row), T), pl.ds(pl.multiple_of(slot * T, T), T)], ar.at[slot],
        )

    @pl.when(a_sender)
    def _():
        a_local().start()

        @pl.loop(0, NZ)
        def _(to):
            @pl.when(to != z)
            def _():
                a_copy(to, col // 2, core).start()

    def top_piece(i):
        return remote(
            mob.at[pl.ds(pl.multiple_of(i * 8, 8), 8), :], top.at[row, i // NY, i % NY], sts.at[i], str_.at[row], (i, col)
        )

    def top_own():
        return pltpu.make_async_copy(
            mob.at[pl.ds(pl.multiple_of(row * 8, 8), 8), :], top.at[row, x, y], loc.at[0]
        )

    def left_piece(i):
        return remote(
            mob.at[pl.ds(pl.multiple_of(i * piece, 8), piece), 0:T],
            left.at[i, :, pl.ds(pl.multiple_of(col * T, T), T)], sls.at[i], slr.at[col], (row, i),
        )

    def left_own():
        return pltpu.make_async_copy(
            mob.at[pl.ds(pl.multiple_of(col * piece, 8), piece), 0:T],
            left.at[col, :, pl.ds(pl.multiple_of(col * T, T), T)], loc.at[1],
        )

    @pl.when(row < NB)
    def _():
        top_own().start()

        @pl.loop(0, R)
        def _(i):
            @pl.when(i != row)
            def _():
                top_piece(i).start()

    @pl.when(col < NB)
    def _():
        left_own().start()

        @pl.loop(0, C)
        def _(i):
            @pl.when(i != col)
            def _():
                left_piece(i).start()

    def b1(r, slot, to):
        ref = sq.at[core, pl.ds(r * T, T), pl.ds(slot * T, T)]
        return remote(ref, ref, b1s.at[slot, to], br.at[r, slot], (to * NY + y, col))

    def b2(r, slot, to):
        ref = sq.at[core, pl.ds(r * T, T), pl.ds(slot * T, T)]
        return remote(ref, ref, b2s.at[r, slot, to], br.at[r, slot], (x * NY + to, col))

    def c_copy(half, r, slot):
        ref = sq.at[half, pl.ds(r * T, T), pl.ds(slot * T, T)]
        return remote(ref, ref, cs.at[r, slot], cr.at[r, slot], (row, other))

    for r in range(NB):
        @pl.when(row == r)
        def _():
            for slot in range(NB // 2):
                @pl.when(2 * slot + core >= r)
                def _():
                    a_copy(z, slot, core).wait_recv()

                    @pl.loop(0, NX)
                    def _(to):
                        @pl.when(to != x)
                        def _():
                            b1(r, slot, to).start()

    def forward(r):
        @pl.when(y == r % NY)
        def _():
            for slot in range(NB // 2):
                @pl.when(2 * slot + core >= r)
                def _():
                    @pl.when(x != r // NY)
                    def _():
                        b1(r, slot, x).wait_recv()

                    @pl.loop(0, NY)
                    def _(to):
                        @pl.when(to != y)
                        def _():
                            b2(r, slot, to).start()

    for r in range(NY):
        forward(r)

    def swap_strip(r):
        for slot in range(NB // 2):
            @pl.when(2 * slot + core >= r)
            def _():
                @pl.when(y != r % NY)
                def _():
                    b2(r, slot, y).wait_recv()

                c_copy(core, r, slot).start()

    def wait_strip(r):
        for slot in range(NB // 2):
            @pl.when(2 * slot + 1 - core >= r)
            def _():
                c_copy(1 - core, r, slot).wait_recv()

    def wait_top():
        for g in range(NB):
            @pl.when(row != g)
            def _():
                ref = top.at[g, x, y]
                remote(ref, ref, sts.at[0], str_.at[g], (row, col)).wait_recv()

        @pl.when(row < NB)
        def _():
            top_own().wait()

    def wait_left():
        for g in range(NB):
            @pl.when(col != g)
            def _():
                ref = left.at[col, :, pl.ds(g * T, T)]
                remote(ref, ref, sls.at[0], slr.at[g], (row, col)).wait_recv()

        @pl.when(col < NB)
        def _():
            left_own().wait()

    H = NB // 2

    def tcopy(phase, axis, kind, at):
        src = (at + (0, 0, 3, 1)[kind]) % 4
        to = (at + (1, 3, 1, 3)[kind]) % 4
        if phase == 0:
            src, to = at, (at + (1, 3, 2)[kind]) % 4
            ref = top.at[0:H, src, y] if axis == 0 else top.at[H:NB, x, src]
        else:
            part = (slice(None), slice(None), slice(0, 2), slice(2, 4))[kind]
            ref = top.at[0:H, part, src] if axis == 1 else top.at[H:NB, src, part]
        device = (to * NY + y, col) if axis == 0 else (x * NY + to, col)
        return remote(ref, ref, ts.at[phase, axis, kind], tr.at[phase, axis, kind], device)

    place = (x, y)

    def kinds(phase):
        return range(3) if phase == 0 else range(4)

    def sender(phase, kind):
        return (3, 1, 2)[kind] if phase == 0 else (3, 1, 3, 1)[kind]

    def spread(phase, step):
        for axis in range(2):
            if step == 1:
                for kind in range(2):
                    tcopy(phase, axis, kind, (place[axis] + sender(phase, kind)) % 4).wait_recv()
            for kind in range(3) if phase == 0 else range(2 * step, 2 * step + 2):
                tcopy(phase, axis, kind, place[axis]).start()

    def spread_end(phase):
        for axis in range(2):
            for kind in range(3) if phase == 0 else range(2, 4):
                tcopy(phase, axis, kind, (place[axis] + sender(phase, kind)) % 4).wait_recv()

    def spread_sent():
        for phase in range(2):
            for axis in range(2):
                for kind in kinds(phase):
                    tcopy(phase, axis, kind, place[axis]).wait_send()

    HOPS = NZ // 2
    part = piece // 16 * 8

    def up(step, at):
        ref = left.at[(at - step + NZ) % NZ * 2 + core]
        if step == HOPS - 1:
            ref = ref.at[0:part]
        return remote(ref, ref, us.at[step], ur.at[step], (row, (z + 1) % NZ * 2 + core))

    def down(step, at):
        ref = left.at[(at + step) % NZ * 2 + core]
        if step == HOPS - 1:
            ref = ref.at[part:piece]
        return remote(ref, ref, ds.at[step], dr.at[step], (row, (z + NZ - 1) % NZ * 2 + core))


    def swap(which, half, zz):
        ref = left.at[zz * 2 + half]
        return remote(ref, ref, ws.at[which], wr.at[which], (row, other))

    def set_of(which):
        if which <= HOPS:
            return (z - which + NZ) % NZ
        return (z + which - HOPS) % NZ

    def hop(step):
        if step > 0:
            up(step - 1, (z - 1 + NZ) % NZ).wait_recv()
        if step < HOPS:
            up(step, z).start()
        if step > 0:
            down(step - 1, (z + 1) % NZ).wait_recv()
        if step < HOPS:
            down(step, z).start()
        swap(step, core, set_of(step)).start()
        if 0 < step < HOPS:
            swap(HOPS + step, core, set_of(HOPS + step)).start()

    y_ref[...] = jnp.zeros_like(y_ref)
    swap_strip(0)

    def tile(r, c):
        return sq.at[c % 2, pl.ds(r * T, T), pl.ds(c // 2 * T, T)]

    @pl.loop(0, NB)
    def _(k):
        for kk in range(NB):
            lo, hi = kk * T, kk * T + T

            @pl.when(k == kk)
            def _():
                wait_strip(kk)
                if kk == 0:
                    d_scr[...] = tile(0, 0)[...]
                else:
                    w = u_scr[:lo, lo:hi]
                    d_scr[...] = tile(kk, kk)[...] - dot_t(w, u_scr[:lo, lo:hi])
                if kk + 1 < NB:
                    swap_strip(kk + 1)
                if kk == 0:
                    forward(4)
                    forward(5)
                if kk == 3:
                    hop(1)
                if kk == 5:
                    spread(1, 1)

        def between():
            for kk in range(NB):
                @pl.when(k == kk)
                def _():
                    if kk == 0:
                        wait_top()
                        spread(0, 0)
                    if kk == 1:
                        wait_left()
                        hop(0)
                    if kk == 2:
                        spread_end(0)
                        spread(1, 0)
                    if kk == 4:
                        hop(2)

        factor_diag(d_scr, v_scr, between)
        for kk in range(NB):
            lo, hi = kk * T, kk * T + T

            @pl.when(k == kk)
            def _():
                inverse = v_scr[...]
                y_ref[lo:hi, lo:hi] = inverse
                if kk > 0:
                    w = u_scr[:lo, lo:hi]
                    y_ref[lo:hi, :lo] = -dot(inverse, dot_t(w, y_ref[:lo, :lo]))
                if hi < B:
                    r = jnp.concatenate([tile(kk, c)[...] for c in range(kk + 1, NB)], axis=1)
                    if kk > 0:
                        r = r - dot_t(w, u_scr[:lo, hi:])
                    u_scr[lo:hi, hi:] = dot(inverse, r)

    pair = 2 * piece

    def rows_of(which):
        return pl.ds(pl.multiple_of(set_of(which) * pair, 8), pair)

    def solve_left(group):
        for which in group:
            swap(which, 1 - core, set_of(which)).wait_recv()
        raw = jnp.concatenate([left[pl.ds(2 * set_of(w), 2)].reshape(pair, B) for w in group], axis=0)
        lh, ll = halves(raw)
        dims = (((1,), (1,)), ((), ()))
        for b in range(B // BLK):
            lo, hi = b * BLK, (b + 1) * BLK
            ih, il = i3[0, lo:hi, :hi], i3[1, lo:hi, :hi]
            s = lax.dot_general(lh[:, :hi], ih, dims, preferred_element_type=F)
            s += lax.dot_general(lh[:, :hi], il, dims, preferred_element_type=F)
            s += lax.dot_general(ll[:, :hi], ih, dims, preferred_element_type=F)
            for n, which in enumerate(group):
                xl[rows_of(which), lo:hi] = s[n * pair : (n + 1) * pair]

    def save_left(which):
        rows = rows_of(which)
        return pltpu.make_async_copy(xl.at[rows, :], xl_out.at[rows, :], os_.at[which])

    hop(3)
    high, low = halves(y_ref[...])
    i3[0] = high
    i3[1] = low
    solve_left((0, 1, 5, 2, 6))
    for which in (0, 1, 5, 2, 6):
        save_left(which).start()

    spread_end(1)
    for g in range(NB):
        high, low = halves(top[g].reshape(T, t3.shape[1]))
        t3[g * T : g * T + T, :] = high
        t3[B + g * T : B + g * T + T, :] = low
    for b in reversed(range(B // BLK)):
        lo, hi = b * BLK, (b + 1) * BLK
        ih, il = i3[0, lo:hi, :hi], i3[1, lo:hi, :hi]
        th, tl = t3[:hi, :], t3[B : B + hi, :]
        s = jnp.dot(ih, th, preferred_element_type=F)
        s += jnp.dot(ih, tl, preferred_element_type=F)
        s += jnp.dot(il, th, preferred_element_type=F)
        high, low = halves(s)
        t3[lo:hi, :] = high
        t3[B + lo : B + hi, :] = low
    save_top = pltpu.make_async_copy(t3, t3_out, loc.at[2])
    save_top.start()
    hop(4)
    solve_left((3, 7, 4))
    for which in (3, 7, 4):
        save_left(which).start()

    @pl.when(a_sender)
    def _():
        @pl.loop(0, NZ)
        def _(to):
            @pl.when(to != z)
            def _():
                a_copy(to, col // 2, core).wait_send()

    for r in range(NB):
        @pl.when(row == r)
        def _():
            for slot in range(NB // 2):
                @pl.when(2 * slot + core >= r)
                def _():
                    @pl.loop(0, NX)
                    def _(to):
                        @pl.when(to != x)
                        def _():
                            b1(r, slot, to).wait_send()

        @pl.when(y == r % NY)
        def _():
            for slot in range(NB // 2):
                @pl.when(2 * slot + core >= r)
                def _():
                    @pl.loop(0, NY)
                    def _(to):
                        @pl.when(to != y)
                        def _():
                            b2(r, slot, to).wait_send()

        for slot in range(NB // 2):
            @pl.when(2 * slot + core >= r)
            def _():
                c_copy(core, r, slot).wait_send()

    @pl.when(row < NB)
    def _():
        @pl.loop(0, R)
        def _(i):
            @pl.when(i != row)
            def _():
                top_piece(i).wait_send()

    @pl.when(col < NB)
    def _():
        @pl.loop(0, C)
        def _(i):
            @pl.when(i != col)
            def _():
                left_piece(i).wait_send()

    spread_sent()
    for step in range(HOPS):
        up(step, z).wait_send()
        down(step, z).wait_send()
    for which in range(NZ):
        swap(which, core, set_of(which)).wait_send()
        save_left(which).wait()
    save_top.wait()


def solve(mobility):
    rows, cols = mobility.shape
    D = pltpu.SemaphoreType.DMA
    return pl.pallas_call(
        panel_kernel,
        out_shape=(jax.ShapeDtypeStruct((2 * B, cols), BF), jax.ShapeDtypeStruct((rows, B), F)),
        in_specs=[pl.BlockSpec(memory_space=pl.ANY)],
        out_specs=(pl.BlockSpec(memory_space=pl.ANY), pl.BlockSpec(memory_space=pl.ANY)),
        scratch_shapes=[
            pltpu.VMEM((NB, NX, NY, T // R, cols), F),
            pltpu.VMEM((C, rows // C, B), F),
            pltpu.VMEM((B, B), F),
            pltpu.VMEM((2, B, B // 2), F),
            pltpu.VMEM((B, B), F),
            pltpu.VMEM((T, T), F),
            pltpu.VMEM((T, T), F),
            pltpu.VMEM((2, B, B), BF),
            pltpu.VMEM((2 * B, cols), BF),
            pltpu.VMEM((rows, B), F),
            D((NZ,)), D((NB // 2,)),
            D((NB // 2, NX)), D((NB, NB // 2, NY)), D((NB, NB // 2)),
            D((NB, NB // 2)), D((NB, NB // 2)),
            D((R,)), D((NB,)), D((C,)), D((NB,)), D((3,)),
            D((2, 2, 4)), D((2, 2, 4)),
            D((4,)), D((4,)), D((4,)), D((4,)), D((NZ,)), D((NZ,)), D((NZ,)),
        ],
        compiler_params=pltpu.CompilerParams(
            collective_id=0, has_side_effects=True, vmem_limit_bytes=52 << 20
        ),
    )(mobility)


def update_kernel(mob, left, t3, out):
    xh, xo = halves(left[...])
    th, tl = t3[:B, :], t3[B:, :]
    s = jnp.dot(xh, th, preferred_element_type=F)
    s += jnp.dot(xh, tl, preferred_element_type=F)
    s += jnp.dot(xo, th, preferred_element_type=F)
    out[...] = mob[...] - s
    col = lax.axis_index("col")

    @pl.when(col < NB)
    def _():
        out[:, 0:T] = left[:, pl.ds(pl.multiple_of(jnp.minimum(col, NB - 1) * T, T), T)]


def on_device(mobility):
    rows, cols = mobility.shape
    top, left = solve(mobility)
    size = rows // STEPS
    return pl.pallas_call(
        update_kernel,
        grid=(STEPS,),
        out_shape=jax.ShapeDtypeStruct(mobility.shape, F),
        in_specs=[
            pl.BlockSpec((size, cols), lambda i: (i, 0)),
            pl.BlockSpec((size, B), lambda i: (i, 0)),
            pl.BlockSpec((2 * B, cols), lambda i: (0, 0)),
        ],
        out_specs=pl.BlockSpec((size, cols), lambda i: (i, 0)),
        compiler_params=pltpu.CompilerParams(vmem_limit_bytes=56 << 20),
    )(mobility, left, top)


def solution(mesh):
    return jax.shard_map(
        on_device,
        mesh=mesh,
        in_specs=(P("row", "col"),),
        out_specs=P("row", "col"),
        check_vma=False,
    )
```

```python
import jax
import jax.numpy as jnp
from jax import lax
from jax.experimental import pallas as pl
from jax.experimental.pallas import tpu as pltpu
from jax.sharding import PartitionSpec as P

B = 768
T = 128
NB = B // T
BLK = 256
STEPS = 4
NX, NY = 4, 4
NZ = 8
R = NX * NY
C = NZ * 2
F = jnp.float32
BF = jnp.bfloat16
MESH = pl.DeviceIdType.MESH
HIGHEST = lax.Precision.HIGHEST


def dot(a, b):
    return lax.dot_general(a, b, (((1,), (0,)), ((), ())), precision=HIGHEST, preferred_element_type=F)


def dot_t(a, b):
    return lax.dot_general(a, b, (((0,), (0,)), ((), ())), precision=HIGHEST, preferred_element_type=F)


def factor_diag(d_ref, v_ref, between):
    sub = lax.broadcasted_iota(jnp.int32, (8, T), 0)

    def wide(x):
        return jnp.broadcast_to(x, (8, T))

    count, group = T // 8, T // 16
    eye = lax.broadcasted_iota(jnp.int32, (T, T), 0) == lax.broadcasted_iota(jnp.int32, (T, T), 1)
    v_ref[...] = jnp.where(eye, 1.0, 0.0).astype(F)
    for first in range(0, count, group):
        end = first + group
        last = end == count
        a = {q: d_ref[8 * q : 8 * q + 8, :] for q in range(first, end)}
        v = {q: v_ref[8 * q : 8 * q + 8, :] for q in range(first, end)}
        done_a, done_v, ahead = [], [], None
        for p in range(first, end):
            c = ahead
            if c is None:
                c = [wide(a[p][:, 8 * p + i : 8 * p + i + 1]) for i in range(8)]
            near, far = p + 1 < end, p + 2 < end
            if near:
                co = [wide(a[p + 1][:, 8 * p + i : 8 * p + i + 1]) for i in range(8)]
                ahead = [wide(a[p + 1][:, 8 * p + 8 + k : 8 * p + 9 + k]) for k in range(8)]
            wa = fa = a[p]
            wv = fv = v[p]
            scale = inverses = None
            for i in range(8):
                here = sub == i
                pivot = wide(c[i][i : i + 1, :])
                inverse = 1.0 / pivot
                m = jnp.where(here, 0.0, c[i]) * inverse
                below = jnp.where(sub > i, c[i], 0.0) * inverse
                for k in range(i + 1, 8):
                    c[k] = c[k] - m * wide(c[k][i : i + 1, :])
                row_a, row_v = wide(fa[i : i + 1, :]), wide(fv[i : i + 1, :])
                if near:
                    t = co[i] * inverse
                    for k in range(8):
                        ahead[k] = ahead[k] - t * wide(co[i][k : k + 1, :])
                    a[p + 1] = a[p + 1] - t * row_a
                    v[p + 1] = v[p + 1] - t * row_v
                    for k in range(i + 1, 8):
                        co[k] = co[k] - co[i] * wide(m[k : k + 1, :])
                if far:
                    wa = wa - m * wide(wa[i : i + 1, :])
                    wv = wv - m * wide(wv[i : i + 1, :])
                fv = fv - below * row_v
                fa = fa - below * row_a
                root = lax.rsqrt(pivot)
                scale = root if scale is None else jnp.where(here, root, scale)
                inverses = inverse if inverses is None else jnp.where(here, inverse, inverses)
            fv = fv * scale
            v_ref[8 * p : 8 * p + 8, :] = fv
            if not last:
                done_a.append(fa * scale)
                done_v.append(fv)
            if not far:
                continue
            wa, wv = wa * inverses, wv * inverses
            rows_a = [wide(wa[i : i + 1, :]) for i in range(8)]
            rows_v = [wide(wv[i : i + 1, :]) for i in range(8)]
            for q in range(p + 2, end):
                cq = [wide(a[q][:, 8 * p + i : 8 * p + i + 1]) for i in range(8)]
                for i in range(8):
                    a[q] = a[q] - cq[i] * rows_a[i]
                    v[q] = v[q] - cq[i] * rows_v[i]
        if not last:
            u, w = jnp.concatenate(done_a, axis=0), jnp.concatenate(done_v, axis=0)
            r = dot_t(u, jnp.concatenate([u, w], axis=1))
            d_ref[8 * end :, :] -= r[8 * end :, :T]
            v_ref[8 * end :, :] -= r[8 * end :, T:]
            between()


def remote(src, dst, send, recv, device):
    return pltpu.make_async_remote_copy(
        src_ref=src, dst_ref=dst, send_sem=send, recv_sem=recv, device_id=device, device_id_type=MESH
    )


def halves(x):
    high = x.astype(BF)
    return high, (x - high.astype(F)).astype(BF)


def panel_kernel(
    mob, t3_out, xl_out, top, left, y_ref, sq, u_scr, d_scr, v_scr, i3, t3, xl,
    as_, ar, b1s, b2s, br, cs, cr, sts, str_, sls, slr, loc, ts, tr, us, ur, ds, dr, ws, wr, os_,
):
    row, col = lax.axis_index("row"), lax.axis_index("col")
    x, y = row // NY, row % NY
    z, core = col // 2, col % 2
    other = z * 2 + 1 - core
    piece = mob.shape[0] // C

    barrier = pltpu.get_barrier_semaphore()

    @pl.loop(0, R)
    def _(i):
        @pl.when(i != row)
        def _():
            pl.semaphore_signal(barrier, inc=1, device_id=(i, col), device_id_type=MESH)

    @pl.loop(0, C)
    def _(i):
        @pl.when(i != col)
        def _():
            pl.semaphore_signal(barrier, inc=1, device_id=(row, i), device_id_type=MESH)

    pl.semaphore_wait(barrier, R + C - 2)

    def a_copy(to, slot, half):
        return remote(
            mob.at[0:T, 0:T], sq.at[half, pl.ds(row_at(row), T), pl.ds(pl.multiple_of(slot * T, T), T)],
            as_.at[to], ar.at[slot], (row, to * 2 + half),
        )

    def row_at(r):
        return pl.multiple_of(r * T, T)

    a_sender = jnp.logical_and(row < NB, jnp.logical_and(col < NB, col >= row))

    def a_local():
        slot = col // 2
        return pltpu.make_async_copy(
            mob.at[0:T, 0:T],
            sq.at[core, pl.ds(row_at(row), T), pl.ds(pl.multiple_of(slot * T, T), T)], ar.at[slot],
        )

    @pl.when(a_sender)
    def _():
        a_local().start()

        @pl.loop(0, NZ)
        def _(to):
            @pl.when(to != z)
            def _():
                a_copy(to, col // 2, core).start()

    def top_piece(i):
        return remote(
            mob.at[pl.ds(pl.multiple_of(i * 8, 8), 8), :], top.at[row, i // NY, i % NY], sts.at[i], str_.at[row], (i, col)
        )

    def top_own():
        return pltpu.make_async_copy(
            mob.at[pl.ds(pl.multiple_of(row * 8, 8), 8), :], top.at[row, x, y], loc.at[0]
        )

    def left_piece(i):
        return remote(
            mob.at[pl.ds(pl.multiple_of(i * piece, 8), piece), 0:T],
            left.at[i, :, pl.ds(pl.multiple_of(col * T, T), T)], sls.at[i], slr.at[col], (row, i),
        )

    def left_own():
        return pltpu.make_async_copy(
            mob.at[pl.ds(pl.multiple_of(col * piece, 8), piece), 0:T],
            left.at[col, :, pl.ds(pl.multiple_of(col * T, T), T)], loc.at[1],
        )

    @pl.when(row < NB)
    def _():
        top_own().start()

        @pl.loop(0, R)
        def _(i):
            @pl.when(i != row)
            def _():
                top_piece(i).start()

    @pl.when(col < NB)
    def _():
        left_own().start()

        @pl.loop(0, C)
        def _(i):
            @pl.when(i != col)
            def _():
                left_piece(i).start()

    def b1(r, slot, to):
        ref = sq.at[core, pl.ds(r * T, T), pl.ds(slot * T, T)]
        return remote(ref, ref, b1s.at[slot, to], br.at[r, slot], (to * NY + y, col))

    def b2(r, slot, to):
        ref = sq.at[core, pl.ds(r * T, T), pl.ds(slot * T, T)]
        return remote(ref, ref, b2s.at[r, slot, to], br.at[r, slot], (x * NY + to, col))

    def c_copy(half, r, slot):
        ref = sq.at[half, pl.ds(r * T, T), pl.ds(slot * T, T)]
        return remote(ref, ref, cs.at[r, slot], cr.at[r, slot], (row, other))

    for r in range(NB):
        @pl.when(row == r)
        def _():
            for slot in range(NB // 2):
                @pl.when(2 * slot + core >= r)
                def _():
                    a_copy(z, slot, core).wait_recv()

                    @pl.loop(0, NX)
                    def _(to):
                        @pl.when(to != x)
                        def _():
                            b1(r, slot, to).start()

    def forward(r):
        @pl.when(y == r % NY)
        def _():
            for slot in range(NB // 2):
                @pl.when(2 * slot + core >= r)
                def _():
                    @pl.when(x != r // NY)
                    def _():
                        b1(r, slot, x).wait_recv()

                    @pl.loop(0, NY)
                    def _(to):
                        @pl.when(to != y)
                        def _():
                            b2(r, slot, to).start()

    for r in range(NY):
        forward(r)

    def swap_strip(r):
        for slot in range(NB // 2):
            @pl.when(2 * slot + core >= r)
            def _():
                @pl.when(y != r % NY)
                def _():
                    b2(r, slot, y).wait_recv()

                c_copy(core, r, slot).start()

    def wait_strip(r):
        for slot in range(NB // 2):
            @pl.when(2 * slot + 1 - core >= r)
            def _():
                c_copy(1 - core, r, slot).wait_recv()

    def wait_top():
        for g in range(NB):
            @pl.when(row != g)
            def _():
                ref = top.at[g, x, y]
                remote(ref, ref, sts.at[0], str_.at[g], (row, col)).wait_recv()

        @pl.when(row < NB)
        def _():
            top_own().wait()

    def wait_left():
        for g in range(NB):
            @pl.when(col != g)
            def _():
                ref = left.at[col, :, pl.ds(g * T, T)]
                remote(ref, ref, sls.at[0], slr.at[g], (row, col)).wait_recv()

        @pl.when(col < NB)
        def _():
            left_own().wait()

    H = NB // 2

    def tcopy(phase, axis, kind, at):
        src = (at + (0, 0, 3, 1)[kind]) % 4
        to = (at + (1, 3, 1, 3)[kind]) % 4
        if phase == 0:
            src, to = at, (at + (1, 3, 2)[kind]) % 4
            ref = top.at[0:H, src, y] if axis == 0 else top.at[H:NB, x, src]
        else:
            part = (slice(None), slice(None), slice(0, 2), slice(2, 4))[kind]
            ref = top.at[0:H, part, src] if axis == 1 else top.at[H:NB, src, part]
        device = (to * NY + y, col) if axis == 0 else (x * NY + to, col)
        return remote(ref, ref, ts.at[phase, axis, kind], tr.at[phase, axis, kind], device)

    place = (x, y)

    def kinds(phase):
        return range(3) if phase == 0 else range(4)

    def sender(phase, kind):
        return (3, 1, 2)[kind] if phase == 0 else (3, 1, 3, 1)[kind]

    def spread(phase, step):
        for axis in range(2):
            if step == 1:
                for kind in range(2):
                    tcopy(phase, axis, kind, (place[axis] + sender(phase, kind)) % 4).wait_recv()
            for kind in range(3) if phase == 0 else range(2 * step, 2 * step + 2):
                tcopy(phase, axis, kind, place[axis]).start()

    def spread_end(phase):
        for axis in range(2):
            for kind in range(3) if phase == 0 else range(2, 4):
                tcopy(phase, axis, kind, (place[axis] + sender(phase, kind)) % 4).wait_recv()

    def spread_sent():
        for phase in range(2):
            for axis in range(2):
                for kind in kinds(phase):
                    tcopy(phase, axis, kind, place[axis]).wait_send()

    HOPS = NZ // 2
    part = piece // 16 * 8

    def up(step, at):
        ref = left.at[(at - step + NZ) % NZ * 2 + core]
        if step == HOPS - 1:
            ref = ref.at[0:part]
        return remote(ref, ref, us.at[step], ur.at[step], (row, (z + 1) % NZ * 2 + core))

    def down(step, at):
        ref = left.at[(at + step) % NZ * 2 + core]
        if step == HOPS - 1:
            ref = ref.at[part:piece]
        return remote(ref, ref, ds.at[step], dr.at[step], (row, (z + NZ - 1) % NZ * 2 + core))


    def swap(which, half, zz):
        ref = left.at[zz * 2 + half]
        return remote(ref, ref, ws.at[which], wr.at[which], (row, other))

    def set_of(which):
        if which <= HOPS:
            return (z - which + NZ) % NZ
        return (z + which - HOPS) % NZ

    def hop(step):
        if step > 0:
            up(step - 1, (z - 1 + NZ) % NZ).wait_recv()
        if step < HOPS:
            up(step, z).start()
        if step > 0:
            down(step - 1, (z + 1) % NZ).wait_recv()
        if step < HOPS:
            down(step, z).start()
        swap(step, core, set_of(step)).start()
        if 0 < step < HOPS:
            swap(HOPS + step, core, set_of(HOPS + step)).start()

    y_ref[...] = jnp.zeros_like(y_ref)
    swap_strip(0)

    def tile(r, c):
        return sq.at[c % 2, pl.ds(r * T, T), pl.ds(c // 2 * T, T)]

    @pl.loop(0, NB)
    def _(k):
        for kk in range(NB):
            lo, hi = kk * T, kk * T + T

            @pl.when(k == kk)
            def _():
                wait_strip(kk)
                if kk == 0:
                    d_scr[...] = tile(0, 0)[...]
                else:
                    w = u_scr[:lo, lo:hi]
                    d_scr[...] = tile(kk, kk)[...] - dot_t(w, u_scr[:lo, lo:hi])
                if kk + 1 < NB:
                    swap_strip(kk + 1)
                if kk == 0:
                    forward(4)
                    forward(5)
                if kk == 3:
                    hop(1)
                if kk == 5:
                    spread(1, 1)

        def between():
            for kk in range(NB):
                @pl.when(k == kk)
                def _():
                    if kk == 0:
                        wait_top()
                        spread(0, 0)
                    if kk == 1:
                        wait_left()
                        hop(0)
                    if kk == 2:
                        spread_end(0)
                        spread(1, 0)
                    if kk == 4:
                        hop(2)

        factor_diag(d_scr, v_scr, between)
        for kk in range(NB):
            lo, hi = kk * T, kk * T + T

            @pl.when(k == kk)
            def _():
                inverse = v_scr[...]
                y_ref[lo:hi, lo:hi] = inverse
                if kk > 0:
                    w = u_scr[:lo, lo:hi]
                    y_ref[lo:hi, :lo] = -dot(inverse, dot_t(w, y_ref[:lo, :lo]))
                if hi < B:
                    r = jnp.concatenate([tile(kk, c)[...] for c in range(kk + 1, NB)], axis=1)
                    if kk > 0:
                        r = r - dot_t(w, u_scr[:lo, hi:])
                    u_scr[lo:hi, hi:] = dot(inverse, r)

    pair = 2 * piece

    def rows_of(which):
        return pl.ds(pl.multiple_of(set_of(which) * pair, 8), pair)

    def solve_left(group):
        for which in group:
            swap(which, 1 - core, set_of(which)).wait_recv()
        raw = jnp.concatenate([left[pl.ds(2 * set_of(w), 2)].reshape(pair, B) for w in group], axis=0)
        lh, ll = halves(raw)
        dims = (((1,), (1,)), ((), ()))
        for b in range(B // BLK):
            lo, hi = b * BLK, (b + 1) * BLK
            ih, il = i3[0, lo:hi, :hi], i3[1, lo:hi, :hi]
            s = lax.dot_general(lh[:, :hi], ih, dims, preferred_element_type=F)
            s += lax.dot_general(lh[:, :hi], il, dims, preferred_element_type=F)
            s += lax.dot_general(ll[:, :hi], ih, dims, preferred_element_type=F)
            for n, which in enumerate(group):
                xl[rows_of(which), lo:hi] = s[n * pair : (n + 1) * pair]

    def save_left(which):
        rows = rows_of(which)
        return pltpu.make_async_copy(xl.at[rows, :], xl_out.at[rows, :], os_.at[which])

    hop(3)
    high, low = halves(y_ref[...])
    i3[0] = high
    i3[1] = low
    solve_left((0, 1, 5, 2, 6))
    for which in (0, 1, 5, 2, 6):
        save_left(which).start()

    spread_end(1)
    for g in range(NB):
        high, low = halves(top[g].reshape(T, t3.shape[1]))
        t3[g * T : g * T + T, :] = high
        t3[B + g * T : B + g * T + T, :] = low
    for b in reversed(range(B // BLK)):
        lo, hi = b * BLK, (b + 1) * BLK
        ih, il = i3[0, lo:hi, :hi], i3[1, lo:hi, :hi]
        th, tl = t3[:hi, :], t3[B : B + hi, :]
        s = jnp.dot(ih, th, preferred_element_type=F)
        s += jnp.dot(ih, tl, preferred_element_type=F)
        s += jnp.dot(il, th, preferred_element_type=F)
        high, low = halves(s)
        t3[lo:hi, :] = high
        t3[B + lo : B + hi, :] = low
    save_top = pltpu.make_async_copy(t3, t3_out, loc.at[2])
    save_top.start()
    hop(4)
    solve_left((3, 7))
    solve_left((4,))
    for which in (3, 7, 4):
        save_left(which).start()

    @pl.when(a_sender)
    def _():
        @pl.loop(0, NZ)
        def _(to):
            @pl.when(to != z)
            def _():
                a_copy(to, col // 2, core).wait_send()

    for r in range(NB):
        @pl.when(row == r)
        def _():
            for slot in range(NB // 2):
                @pl.when(2 * slot + core >= r)
                def _():
                    @pl.loop(0, NX)
                    def _(to):
                        @pl.when(to != x)
                        def _():
                            b1(r, slot, to).wait_send()

        @pl.when(y == r % NY)
        def _():
            for slot in range(NB // 2):
                @pl.when(2 * slot + core >= r)
                def _():
                    @pl.loop(0, NY)
                    def _(to):
                        @pl.when(to != y)
                        def _():
                            b2(r, slot, to).wait_send()

        for slot in range(NB // 2):
            @pl.when(2 * slot + core >= r)
            def _():
                c_copy(core, r, slot).wait_send()

    @pl.when(row < NB)
    def _():
        @pl.loop(0, R)
        def _(i):
            @pl.when(i != row)
            def _():
                top_piece(i).wait_send()

    @pl.when(col < NB)
    def _():
        @pl.loop(0, C)
        def _(i):
            @pl.when(i != col)
            def _():
                left_piece(i).wait_send()

    spread_sent()
    for step in range(HOPS):
        up(step, z).wait_send()
        down(step, z).wait_send()
    for which in range(NZ):
        swap(which, core, set_of(which)).wait_send()
        save_left(which).wait()
    save_top.wait()


def solve(mobility):
    rows, cols = mobility.shape
    D = pltpu.SemaphoreType.DMA
    return pl.pallas_call(
        panel_kernel,
        out_shape=(jax.ShapeDtypeStruct((2 * B, cols), BF), jax.ShapeDtypeStruct((rows, B), F)),
        in_specs=[pl.BlockSpec(memory_space=pl.ANY)],
        out_specs=(pl.BlockSpec(memory_space=pl.ANY), pl.BlockSpec(memory_space=pl.ANY)),
        scratch_shapes=[
            pltpu.VMEM((NB, NX, NY, T // R, cols), F),
            pltpu.VMEM((C, rows // C, B), F),
            pltpu.VMEM((B, B), F),
            pltpu.VMEM((2, B, B // 2), F),
            pltpu.VMEM((B, B), F),
            pltpu.VMEM((T, T), F),
            pltpu.VMEM((T, T), F),
            pltpu.VMEM((2, B, B), BF),
            pltpu.VMEM((2 * B, cols), BF),
            pltpu.VMEM((rows, B), F),
            D((NZ,)), D((NB // 2,)),
            D((NB // 2, NX)), D((NB, NB // 2, NY)), D((NB, NB // 2)),
            D((NB, NB // 2)), D((NB, NB // 2)),
            D((R,)), D((NB,)), D((C,)), D((NB,)), D((3,)),
            D((2, 2, 4)), D((2, 2, 4)),
            D((4,)), D((4,)), D((4,)), D((4,)), D((NZ,)), D((NZ,)), D((NZ,)),
        ],
        compiler_params=pltpu.CompilerParams(
            collective_id=0, has_side_effects=True, vmem_limit_bytes=52 << 20
        ),
    )(mobility)


def update_kernel(mob, left, t3, out):
    xh, xo = halves(left[...])
    th, tl = t3[:B, :], t3[B:, :]
    s = jnp.dot(xh, th, preferred_element_type=F)
    s += jnp.dot(xh, tl, preferred_element_type=F)
    s += jnp.dot(xo, th, preferred_element_type=F)
    out[...] = mob[...] - s
    col = lax.axis_index("col")

    @pl.when(col < NB)
    def _():
        out[:, 0:T] = left[:, pl.ds(pl.multiple_of(jnp.minimum(col, NB - 1) * T, T), T)]


def on_device(mobility):
    rows, cols = mobility.shape
    top, left = solve(mobility)
    size = rows // STEPS
    return pl.pallas_call(
        update_kernel,
        grid=(STEPS,),
        out_shape=jax.ShapeDtypeStruct(mobility.shape, F),
        in_specs=[
            pl.BlockSpec((size, cols), lambda i: (i, 0)),
            pl.BlockSpec((size, B), lambda i: (i, 0)),
            pl.BlockSpec((2 * B, cols), lambda i: (0, 0)),
        ],
        out_specs=pl.BlockSpec((size, cols), lambda i: (i, 0)),
        compiler_params=pltpu.CompilerParams(vmem_limit_bytes=56 << 20),
    )(mobility, left, top)


def solution(mesh):
    return jax.shard_map(
        on_device,
        mesh=mesh,
        in_specs=(P("row", "col"),),
        out_specs=P("row", "col"),
        check_vma=False,
    )
```
